512 devices in a mesh: sec: 16 (over y, core), cp: 32 (over x, z).
Axes of the slice: x: 4, y: 8, z: 8, core: 2. Of those that a mesh axis runs over, the one named last changes fastest.
Arguments:
- projected: bfloat16 [65536, 10240], P(('sec', 'cp')), may hold values from -6 to 6
- conv_weight: float32 [4, 10240], replicated, may hold values from -3 to 3
- conv_bias: float32 [10240], replicated, may hold values from -3 to 3
- step_size: bfloat16 [65536, 128], P(('sec', 'cp')), may hold values from 0 to 1
- log_decay: bfloat16 [65536, 128], P(('sec', 'cp')), may hold values from -1 to 0
- skip_gain: float32 [128], replicated, may hold values from 0.5 to 1.5
Outputs:
- ssd_out: bfloat16 [65536, 8192], P(('sec', 'cp'))
The draws below stay inside these ranges and needn't reach their ends.
All inputs are finite; a program needn't handle non-finite values.
Results may differ from the reference program's by a relative error of at most 0.0034.
Values may be sent and summed in bfloat16 or wider, within the bound.
No kernel may reach another device: no remote copies, remote signals or barrier semaphores. Data moves between devices by JAX's collectives and lax.ppermute only.
A program may use at most 64 MiB of HBM per device.

```python
import math
import jax
import jax.numpy as jnp
from jax import lax

HEAD_COUNT = 128
P_SIZE = 64
N = 128
G = 8
BLOCK = 256
KERNEL = 4
CH = 10240
SEQUENCE_TOKENS = 65536


def decay_and_steps(key):
    head_key = jax.random.fold_in(key, 101)
    fast_key = jax.random.fold_in(key, 102)
    slow_key = jax.random.fold_in(key, 103)
    rough_key = jax.random.fold_in(key, 104)
    spike_random_key = jax.random.fold_in(key, 105)
    amount_random_key = jax.random.fold_in(key, 106)
    step_key = jax.random.fold_in(key, 107)
    fast_share = 0.4
    head_draw = jax.random.uniform(head_key, (HEAD_COUNT,), jnp.float32)
    fast_rates = jnp.exp(jax.random.uniform(fast_key, (HEAD_COUNT,), jnp.float32, math.log(1.0 / 50.0), math.log(1.0 / 30.0)))
    slow_rates = jnp.exp(jax.random.uniform(slow_key, (HEAD_COUNT,), jnp.float32, math.log(0.2), math.log(0.8))) / SEQUENCE_TOKENS
    baseline_rate = jnp.where(head_draw < fast_share, fast_rates, slow_rates)
    jaggedness = jnp.exp(jax.random.uniform(rough_key, (SEQUENCE_TOKENS, HEAD_COUNT), jnp.float32, math.log(0.5), math.log(2.0)))
    spike_mask = jax.random.uniform(spike_random_key, (SEQUENCE_TOKENS, HEAD_COUNT), jnp.float32) < 2.0 / SEQUENCE_TOKENS
    spike_magnitude = jax.random.uniform(amount_random_key, (SEQUENCE_TOKENS, HEAD_COUNT), jnp.float32, 0.22, 0.69)
    combined_rate = baseline_rate[None, :] * jaggedness + jnp.where(spike_mask, spike_magnitude, 0.0)
    step_values = jnp.sqrt(baseline_rate / 8.0)[None, :] * jnp.exp(jax.random.uniform(step_key, (SEQUENCE_TOKENS, HEAD_COUNT), jnp.float32, math.log(0.5), math.log(2.0)))
    return (-combined_rate, step_values)


def draw_log_decay(key, part):
    return decay_and_steps(key)[0].astype(jnp.bfloat16)


def draw_step_size(key, part):
    return decay_and_steps(key)[1].astype(jnp.bfloat16)


def level_of(stream_key, shape, pieces, smallest, high):
    factor_of = 1.0
    for axis_at, blocks in pieces:
        steps = jax.random.uniform(jax.random.fold_in(jax.random.fold_in(stream_key, 6), axis_at), (blocks,), jnp.float32, smallest / len(pieces), high / len(pieces))
        factor_of = factor_of * jnp.repeat(jnp.exp(steps), shape[axis_at] // blocks).reshape((-1,) + (1,) * (len(shape) - 1 - axis_at))
    return factor_of


def bell_draw(key, dims, scale, most, pieces=(), kind=jnp.bfloat16):
    values = scale * jax.random.normal(key, dims, jnp.float32)
    if pieces:
        values = values * level_of(key, dims, pieces, -0.22, 0.18)
    return jnp.clip(values, -most, most).astype(kind)


def setup_inputs(seed: int = 0) -> dict:
    keys = jax.random.split(jax.random.key(seed), 7)
    projected = bell_draw(keys[0], (SEQUENCE_TOKENS, CH), 1.0, 6.0, ((0, 512),))
    conv_weight = bell_draw(keys[1], (KERNEL, CH), KERNEL ** -0.5, 3.0, (), jnp.float32)
    conv_bias = bell_draw(keys[2], (CH,), 0.5, 3.0, (), jnp.float32)
    step_size = draw_step_size(jax.random.fold_in(keys[6], 71), 0)
    log_decay = draw_log_decay(jax.random.fold_in(keys[6], 71), 0)
    skip_gain = jnp.clip(jax.random.uniform(keys[5], (HEAD_COUNT,), jnp.float32, 0.5, 1.5), 0.5, 1.5)
    return {"projected": projected, "conv_weight": conv_weight, "conv_bias": conv_bias, "step_size": step_size, "log_decay": log_decay, "skip_gain": skip_gain}


def causal_conv(columns, weights, biases):
    padded = jnp.concatenate([jnp.zeros((KERNEL - 1, columns.shape[1]), columns.dtype), columns], 0)
    length = columns.shape[0]
    summed = biases[None, :] + weights[0][None, :] * padded[0:length].astype(jnp.float32)
    for offset in range(1, KERNEL):
        summed = summed + weights[offset][None, :] * padded[offset:offset + length].astype(jnp.float32)
    return jax.nn.silu(summed).astype(jnp.bfloat16)


def head_output(head_index, projected, conv_weight, conv_bias, step_size, log_decay, skip_gain):
    group_index = head_index // (HEAD_COUNT // G)
    start_x = head_index * P_SIZE
    start_b = HEAD_COUNT * P_SIZE + group_index * N
    start_c = HEAD_COUNT * P_SIZE + G * N + group_index * N
    columns = jnp.concatenate([lax.dynamic_slice_in_dim(projected, start_x, P_SIZE, 1),
                               lax.dynamic_slice_in_dim(projected, start_b, N, 1),
                               lax.dynamic_slice_in_dim(projected, start_c, N, 1)], 1)
    weights = jnp.concatenate([lax.dynamic_slice_in_dim(conv_weight, start_x, P_SIZE, 1),
                               lax.dynamic_slice_in_dim(conv_weight, start_b, N, 1),
                               lax.dynamic_slice_in_dim(conv_weight, start_c, N, 1)], 1)
    biases = jnp.concatenate([lax.dynamic_slice_in_dim(conv_bias, start_x, P_SIZE, 0),
                              lax.dynamic_slice_in_dim(conv_bias, start_b, N, 0),
                              lax.dynamic_slice_in_dim(conv_bias, start_c, N, 0)], 0)
    convolved = causal_conv(columns, weights, biases)
    blocks = SEQUENCE_TOKENS // BLOCK
    values = convolved[:, :P_SIZE].reshape(blocks, BLOCK, P_SIZE)
    keys_b = convolved[:, P_SIZE:P_SIZE + N].reshape(blocks, BLOCK, N)
    query_c = convolved[:, P_SIZE + N:].reshape(blocks, BLOCK, N)
    decay_log = lax.dynamic_slice_in_dim(log_decay, head_index, 1, 1)[:, 0].astype(jnp.float32).reshape(blocks, BLOCK)
    steps_f = lax.dynamic_slice_in_dim(step_size, head_index, 1, 1)[:, 0].astype(jnp.float32).reshape(blocks, BLOCK)
    running = jnp.cumsum(decay_log, axis=1)
    block_end = running[:, -1:]
    weighted_b = (keys_b.astype(jnp.float32) * (jnp.exp(block_end - running) * steps_f)[:, :, None]).astype(jnp.bfloat16)
    block_states = jnp.einsum('csn,csp->cnp', weighted_b.astype(jnp.float32), values.astype(jnp.float32))
    block_gain = jnp.exp(block_end[:, 0])

    def advance(carried, inputs_now):
        add_state, gain_now = inputs_now
        return gain_now * carried + add_state, carried

    _, entering = lax.scan(advance, jnp.zeros((N, P_SIZE), jnp.float32), (block_states, block_gain))
    causal_mask = lax.broadcasted_iota(jnp.int32, (BLOCK, BLOCK), 0) >= lax.broadcasted_iota(jnp.int32, (BLOCK, BLOCK), 1)
    scores = jnp.einsum('ctn,csn->cts', query_c.astype(jnp.float32), keys_b.astype(jnp.float32))
    log_gap = jnp.where(causal_mask[None], running[:, :, None] - running[:, None, :], -jnp.inf)
    mix_weights = (scores * jnp.exp(log_gap) * steps_f[:, None, :]).astype(jnp.bfloat16)
    within = jnp.einsum('cts,csp->ctp', mix_weights.astype(jnp.float32), values.astype(jnp.float32))
    carried_part = jnp.einsum('ctn,cnp->ctp', query_c.astype(jnp.float32), entering,
                              precision=lax.Precision.HIGHEST) * jnp.exp(running)[:, :, None]
    skip_here = lax.dynamic_slice_in_dim(skip_gain, head_index, 1, 0)
    result = (within + carried_part + skip_here * values.astype(jnp.float32)).astype(jnp.bfloat16)
    return result.reshape(SEQUENCE_TOKENS, P_SIZE)


def reference(projected, conv_weight, conv_bias, step_size, log_decay, skip_gain):
    def one_head(head_index, buffer):
        head_index = jnp.asarray(head_index).astype(jnp.int32)
        result = head_output(head_index, projected, conv_weight, conv_bias, step_size, log_decay, skip_gain)
        return lax.dynamic_update_slice_in_dim(buffer, result, head_index * P_SIZE, 1)

    return lax.fori_loop(0, HEAD_COUNT, one_head, jnp.zeros((SEQUENCE_TOKENS, HEAD_COUNT * P_SIZE), jnp.bfloat16))
```

```python
import jax
import jax.numpy as jnp
from jax import lax
from jax.experimental import pallas as pl
from jax.experimental.pallas import tpu as pltpu
from jax.sharding import PartitionSpec as P

HEAD_COUNT = 128
P_SIZE = 64
N = 128
G = 8
KERNEL = 4
GROUP_HEADS = HEAD_COUNT // G
GROUP_WIDTH = GROUP_HEADS * P_SIZE
WIDTH_X = HEAD_COUNT * P_SIZE
F32 = jnp.float32
BF16 = jnp.bfloat16


def lower_ones(rows):
    down = lax.broadcasted_iota(jnp.int32, (rows, rows), 0)
    across = lax.broadcasted_iota(jnp.int32, (rows, rows), 1)
    return down >= across


def dot(a, b, a_dim, b_dim):
    return lax.dot_general(a, b, (((a_dim,), (b_dim,)), ((), ())), preferred_element_type=F32)


def running_sum(decay):
    return dot(lower_ones(decay.shape[0]).astype(BF16), decay, 1, 0)


def over_heads(columns):
    rows = columns.shape[0]
    left = lax.broadcasted_iota(jnp.int32, (rows, 2 * P_SIZE), 1) < P_SIZE
    return jnp.concatenate(
        [
            jnp.where(left, columns[:, h : h + 1], columns[:, h + 1 : h + 2])
            for h in range(0, columns.shape[1], 2)
        ],
        axis=1,
    )


def conv_silu(columns, rim, weights, biases, pad):
    rows = columns.shape[0]
    width = columns.shape[1]
    pad[8 - (KERNEL - 1) : 8, 0:width] = rim.astype(F32)
    pad[8 : 8 + rows, 0:width] = columns.astype(F32)
    summed = biases
    for tap in range(KERNEL):
        first = 8 - (KERNEL - 1) + tap
        summed = summed + weights[tap : tap + 1, :] * pad[first : first + rows, 0:width]
    return (summed / (1.0 + jnp.exp(-summed))).astype(BF16)


def conv_states_kernel(
    x_in, b_in, c_in, x_rim, b_rim, c_rim, x_w, b_w, c_w, x_bias, b_bias, c_bias, step, decay,
    x_out, b_out, c_out, states, pad,
):
    values = conv_silu(x_in[...], x_rim[...], x_w[...], x_bias[...], pad)
    keys_b = conv_silu(b_in[...], b_rim[...], b_w[...], b_bias[...], pad)
    query_c = conv_silu(c_in[...], c_rim[...], c_w[...], c_bias[...], pad)
    x_out[...] = values
    b_out[...] = keys_b
    c_out[...] = query_c
    running = running_sum(decay[0])
    rows = running.shape[0]
    weight = jnp.exp(running[rows - 1 : rows, :] - running) * step[0].astype(F32)
    weighted = (values.astype(F32) * over_heads(weight)).astype(BF16)
    targets, _, width = states.shape
    for target in range(targets):
        states[target] = dot(
            keys_b, weighted[:, target * width : (target + 1) * width], 0, 0
        ).astype(BF16)


def within_kernel(x_in, b_in, c_in, step_t, decay, decay_t, skip, out):
    scores = dot(c_in[...], b_in[...], 1, 1)
    causal = lower_ones(scores.shape[0])
    running = running_sum(decay[0])
    running_t = dot(decay_t[0], causal.astype(BF16), 1, 1)
    steps = step_t[0].astype(F32)
    scores = jnp.where(causal, scores, 0.0)
    for pair in range(GROUP_HEADS // 2):
        parts = []
        x_pair = x_in[:, pair * 2 * P_SIZE : (pair + 1) * 2 * P_SIZE]
        for h in (2 * pair, 2 * pair + 1):
            gap = jnp.where(causal, running[:, h : h + 1] - running_t[h : h + 1, :], -jnp.inf)
            mix = (scores * jnp.exp(gap) * steps[h : h + 1, :]).astype(BF16)
            parts.append(dot(mix, x_pair[:, (h % 2) * P_SIZE : (h % 2 + 1) * P_SIZE], 1, 0))
        at = slice(pair * 2 * P_SIZE, (pair + 1) * 2 * P_SIZE)
        out[:, at] = jnp.concatenate(parts, axis=1) + skip[:, at] * x_pair.astype(F32)


def section_total_kernel(states, gains, total):
    chunks = states.shape[0]
    for part in range(N // 32):
        at = slice(part * 32, (part + 1) * 32)
        carried = states[0, at, :].astype(F32)
        for chunk in range(1, chunks):
            carried = gains[chunk : chunk + 1, :] * carried + states[chunk, at, :].astype(F32)
        total[at, :] = carried


def entering_kernel(states, gains, totals, section_gains, entering):
    chunks = states.shape[0]
    sections = totals.shape[0]
    for part in range(N // 32):
        at = slice(part * 32, (part + 1) * 32)
        carried = section_gains[0:1, :] * totals[0, at, :].astype(F32)
        for section in range(1, sections):
            carried = carried + section_gains[section : section + 1, :] * totals[
                section, at, :
            ].astype(F32)
        for chunk in range(chunks):
            entering[chunk, at, :] = carried.astype(BF16)
            carried = gains[chunk : chunk + 1, :] * carried + states[chunk, at, :].astype(F32)


def outputs_kernel(within, c_in, decay, entering, out):
    growth = over_heads(jnp.exp(running_sum(decay[0])))
    query_c = c_in[...]
    targets, _, width = entering.shape
    for target in range(targets):
        at = slice(target * width, (target + 1) * width)
        out[:, at] = (within[:, at] + growth[:, at] * dot(query_c, entering[target], 1, 0)).astype(
            BF16
        )


def whole(shape):
    return pl.BlockSpec(shape, lambda g: (0,) * len(shape))


def per_device(projected, conv_weight, conv_bias, step_size, log_decay, skip_gain):
    targets = lax.axis_size("cp")
    sections = lax.axis_size("sec")
    rows = projected.shape[0]
    width_all = projected.shape[1]
    heads_here = HEAD_COUNT // targets
    width_here = heads_here * P_SIZE
    group_targets = targets // G
    devices = targets * sections

    rim = lax.ppermute(
        projected[rows - (KERNEL - 1) :],
        ("sec", "cp"),
        [(source, source + 1) for source in range(devices - 1)],
    )
    chunk_decay = jnp.sum(log_decay.astype(F32), axis=0, keepdims=True)
    all_decay = lax.all_gather(chunk_decay, ("sec", "cp"), axis=0, tiled=True)

    decay_g = log_decay.reshape(rows, G, GROUP_HEADS).transpose(1, 0, 2)
    step_g = step_size.reshape(rows, G, GROUP_HEADS).transpose(1, 0, 2)
    decay_t = log_decay.T.reshape(G, GROUP_HEADS, rows)
    step_t = step_size.T.reshape(G, GROUP_HEADS, rows)
    bias = conv_bias.reshape(1, width_all)
    skip_wide = jnp.repeat(skip_gain, P_SIZE).reshape(1, WIDTH_X)

    b_first = WIDTH_X // N
    c_first = b_first + G

    def x_spec(height):
        return pl.BlockSpec((height, GROUP_WIDTH), lambda g: (0, g))

    def bc_spec(height, first=0):
        return pl.BlockSpec((height, N), lambda g: (0, first + g))

    def three(height):
        return [x_spec(height), bc_spec(height, b_first), bc_spec(height, c_first)]

    head_spec = pl.BlockSpec((1, rows, GROUP_HEADS), lambda g: (g, 0, 0))
    head_t_spec = pl.BlockSpec((1, GROUP_HEADS, rows), lambda g: (g, 0, 0))
    states_spec = pl.BlockSpec((group_targets, N, width_here), lambda g: (g, 0, 0))
    params = pltpu.CompilerParams(vmem_limit_bytes=48 * 2**20)

    values, keys_b, query_c, states = pl.pallas_call(
        conv_states_kernel,
        grid=(G,),
        in_specs=three(rows) + three(KERNEL - 1) + three(KERNEL) + three(1) + [head_spec, head_spec],
        out_specs=[x_spec(rows), bc_spec(rows), bc_spec(rows), states_spec],
        out_shape=[
            jax.ShapeDtypeStruct((rows, WIDTH_X), BF16),
            jax.ShapeDtypeStruct((rows, G * N), BF16),
            jax.ShapeDtypeStruct((rows, G * N), BF16),
            jax.ShapeDtypeStruct((targets, N, width_here), BF16),
        ],
        scratch_shapes=[pltpu.VMEM((rows + 8, GROUP_WIDTH), F32)],
        compiler_params=params,
        name="conv_states",
    )(
        projected, projected, projected, rim, rim, rim, conv_weight, conv_weight, conv_weight,
        bias, bias, bias, step_g, decay_g,
    )

    states_here = lax.all_to_all(states, "cp", split_axis=0, concat_axis=0, tiled=True)

    within = pl.pallas_call(
        within_kernel,
        grid=(G,),
        in_specs=[x_spec(rows), bc_spec(rows), bc_spec(rows), head_t_spec, head_spec, head_t_spec, x_spec(1)],
        out_specs=x_spec(rows),
        out_shape=jax.ShapeDtypeStruct((rows, WIDTH_X), F32),
        compiler_params=params,
        name="within",
    )(values, keys_b, query_c, step_t, decay_g, decay_t, skip_wide)

    section = lax.axis_index("sec")
    position = lax.axis_index("cp")
    decay_here = lax.dynamic_slice_in_dim(all_decay, position * heads_here, heads_here, 1)
    decay_here = decay_here.reshape(sections, targets, heads_here)
    chunk_gain = jnp.exp(lax.dynamic_index_in_dim(decay_here, section, 0, keepdims=False))
    chunk_gain = jnp.repeat(chunk_gain, P_SIZE, axis=1)
    section_decay = jnp.sum(decay_here, axis=1)
    earlier = lax.broadcasted_iota(jnp.int32, (sections, sections), 0)
    later = lax.broadcasted_iota(jnp.int32, (sections, sections), 1)
    between = (later > earlier) & (later < section)
    section_gap = jnp.sum(jnp.where(between[:, :, None], section_decay[None], 0.0), axis=1)
    before = lax.broadcasted_iota(jnp.int32, (sections, 1), 0) < section
    section_gain = jnp.where(before, jnp.exp(section_gap), 0.0)
    section_gain = jnp.repeat(section_gain, P_SIZE, axis=1)

    total = pl.pallas_call(
        section_total_kernel,
        out_shape=jax.ShapeDtypeStruct((N, width_here), F32),
        compiler_params=params,
        name="section_total",
    )(states_here, chunk_gain)
    totals = lax.all_gather(total, "sec")
    entering = pl.pallas_call(
        entering_kernel,
        out_shape=jax.ShapeDtypeStruct((targets, N, width_here), BF16),
        compiler_params=params,
        name="entering",
    )(states_here, chunk_gain, totals, section_gain)

    entering_all = lax.all_to_all(entering, "cp", split_axis=0, concat_axis=0, tiled=True)

    return pl.pallas_call(
        outputs_kernel,
        grid=(G,),
        in_specs=[x_spec(rows), bc_spec(rows), head_spec, states_spec],
        out_specs=x_spec(rows),
        out_shape=jax.ShapeDtypeStruct((rows, WIDTH_X), BF16),
        compiler_params=params,
        name="outputs",
    )(within, query_c, decay_g, entering_all)


def solution(mesh):
    in_specs = (
        P(("sec", "cp"), None),
        P(),
        P(),
        P(("sec", "cp"), None),
        P(("sec", "cp"), None),
        P(),
    )
    out_specs = P(("sec", "cp"), None)
    return jax.shard_map(
        per_device, mesh=mesh, in_specs=in_specs, out_specs=out_specs, check_vma=False
    )
```

```python
import functools

import jax
import jax.numpy as jnp
from jax import lax
from jax.experimental import pallas as pl
from jax.experimental.pallas import tpu as pltpu
from jax.sharding import PartitionSpec as P

HEAD_COUNT = 128
P_SIZE = 64
N = 128
G = 8
KERNEL = 4
GROUP_HEADS = HEAD_COUNT // G
GROUP_WIDTH = GROUP_HEADS * P_SIZE
WIDTH_X = HEAD_COUNT * P_SIZE
F32 = jnp.float32
BF16 = jnp.bfloat16
HALVES = 2


def lower_ones(rows):
    down = lax.broadcasted_iota(jnp.int32, (rows, rows), 0)
    across = lax.broadcasted_iota(jnp.int32, (rows, rows), 1)
    return down >= across


def dot(a, b, a_dim, b_dim):
    return lax.dot_general(a, b, (((a_dim,), (b_dim,)), ((), ())), preferred_element_type=F32)


def running_sum(decay):
    return dot(lower_ones(decay.shape[0]).astype(BF16), decay, 1, 0)


def group_columns(columns, group):
    heads = columns.shape[1]
    return pltpu.roll(columns, lax.rem(heads - group * GROUP_HEADS, heads), 1)[:, :GROUP_HEADS]


def over_heads(columns):
    rows = columns.shape[0]
    left = lax.broadcasted_iota(jnp.int32, (rows, 2 * P_SIZE), 1) < P_SIZE
    return jnp.concatenate(
        [
            jnp.where(left, columns[:, h : h + 1], columns[:, h + 1 : h + 2])
            for h in range(0, columns.shape[1], 2)
        ],
        axis=1,
    )


def conv_silu(columns, rim, weights, biases, pad):
    rows = columns.shape[0]
    width = columns.shape[1]
    pad[8 - (KERNEL - 1) : 8, 0:width] = rim.astype(F32)
    pad[8 : 8 + rows, 0:width] = columns.astype(F32)
    summed = biases
    for tap in range(KERNEL):
        first = 8 - (KERNEL - 1) + tap
        summed = summed + weights[tap : tap + 1, :] * pad[first : first + rows, 0:width]
    return (summed / (1.0 + jnp.exp(-summed))).astype(BF16)


def conv_states_kernel(
    first_group, x_in, b_in, c_in, x_rim, b_rim, c_rim, x_w, b_w, c_w, x_bias, b_bias, c_bias, step, decay,
    x_out, b_out, c_out, states, pad,
):
    values = conv_silu(x_in[...], x_rim[...], x_w[...], x_bias[...], pad)
    keys_b = conv_silu(b_in[...], b_rim[...], b_w[...], b_bias[...], pad)
    query_c = conv_silu(c_in[...], c_rim[...], c_w[...], c_bias[...], pad)
    x_out[...] = values
    b_out[...] = keys_b
    c_out[...] = query_c
    group = first_group + pl.program_id(0)
    rows = x_in.shape[0]
    running = group_columns(running_sum(decay[...]), group)
    steps = group_columns(step[...].astype(F32), group)
    weight = jnp.exp(running[rows - 1 : rows, :] - running) * steps
    weighted = (values.astype(F32) * over_heads(weight)).astype(BF16)
    targets, _, width = states.shape
    total = over_heads(running[rows - 1 : rows, :])
    high = total.astype(BF16).astype(F32)
    middle = (total - high).astype(BF16).astype(F32)
    row = lax.broadcasted_iota(jnp.int32, (8, total.shape[1]), 0)
    pieces = jnp.where(row == 0, high, jnp.where(row == 1, middle, total - high - middle))
    pieces = jnp.where(row < 3, pieces, 0.0).astype(BF16)
    for target in range(targets):
        at = slice(target * width, (target + 1) * width)
        states[target, 0:N, :] = dot(keys_b, weighted[:, at], 0, 0).astype(BF16)
        states[target, N : N + 8, :] = pieces[:, at]


def within_kernel(first_group, x_in, b_in, c_in, step, decay, skip, out, running_all, steps_all):
    scores = dot(c_in[...], b_in[...], 1, 1)
    causal = lower_ones(scores.shape[0])
    @pl.when(pl.program_id(0) == 0)
    def _():
        running_all[...] = dot(decay[...], causal.astype(BF16), 0, 1)
        steps_all[...] = step[...].astype(F32).T

    group = first_group + pl.program_id(0)
    running = group_columns(running_sum(decay[...]), group)
    heads = pl.ds(pl.multiple_of(group * GROUP_HEADS, GROUP_HEADS), GROUP_HEADS)
    running_t = running_all[heads, :]
    steps = steps_all[heads, :]
    scores = jnp.where(causal, scores, 0.0)
    for pair in range(GROUP_HEADS // 2):
        parts = []
        x_pair = x_in[:, pair * 2 * P_SIZE : (pair + 1) * 2 * P_SIZE]
        for h in (2 * pair, 2 * pair + 1):
            gap = jnp.where(causal, running[:, h : h + 1] - running_t[h : h + 1, :], -jnp.inf)
            mix = (scores * jnp.exp(gap) * steps[h : h + 1, :]).astype(BF16)
            parts.append(dot(mix, x_pair[:, (h % 2) * P_SIZE : (h % 2 + 1) * P_SIZE], 1, 0))
        at = slice(pair * 2 * P_SIZE, (pair + 1) * 2 * P_SIZE)
        out[:, at] = jnp.concatenate(parts, axis=1) + skip[:, at] * x_pair.astype(F32)


def chunk_decays(states):
    return jnp.sum(states[:, N : N + 8, :].astype(F32), axis=1)


def section_total_kernel(states, total):
    chunks = states.shape[0]
    decays = chunk_decays(states)
    gains = jnp.exp(decays)
    for part in range(N // 32):
        at = slice(part * 32, (part + 1) * 32)
        carried = states[0, at, :].astype(F32)
        for chunk in range(1, chunks):
            carried = gains[chunk : chunk + 1, :] * carried + states[chunk, at, :].astype(F32)
        total[at, :] = carried
    total[N : N + 8, :] = jnp.broadcast_to(
        jnp.sum(decays, axis=0, keepdims=True), (8, total.shape[1])
    )


def entering_kernel(states, carried_in, entering):
    chunks = states.shape[0]
    gains = jnp.exp(chunk_decays(states))
    for part in range(N // 32):
        at = slice(part * 32, (part + 1) * 32)
        carried = carried_in[at, :]
        for chunk in range(chunks):
            entering[chunk, at, :] = carried.astype(BF16)
            carried = gains[chunk : chunk + 1, :] * carried + states[chunk, at, :].astype(F32)


def outputs_kernel(first_group, within, c_in, decay, entering, *rest):
    out = rest[-1]
    group = first_group + pl.program_id(0)
    growth = over_heads(jnp.exp(group_columns(running_sum(decay[...]), group)))
    query_c = c_in[...]
    targets, _, width = entering.shape
    for target in range(targets):
        at = slice(target * width, (target + 1) * width)
        out[:, at] = (within[:, at] + growth[:, at] * dot(query_c, entering[target], 1, 0)).astype(
            BF16
        )


def join_kernel(got, before, through, before_out, through_out):
    for later, out in ((before, before_out), (through, through_out)):
        out[0:N, :] = jnp.exp(later[N : N + 1, :]) * got[0:N, :] + later[0:N, :]
        out[N : N + 8, :] = got[N : N + 8, :] + later[N : N + 8, :]


def before_section(total, params):
    sections = lax.axis_size("sec")
    join = pl.pallas_call(
        join_kernel,
        out_shape=[jax.ShapeDtypeStruct(total.shape, F32)] * 2,
        compiler_params=params,
        name="join",
    )
    through = total
    before = jnp.zeros_like(total)
    steps = 1
    while steps < sections:
        got = lax.ppermute(
            through, "sec", [(source, source + steps) for source in range(sections - steps)]
        )
        before, through = join(got, before, through)
        steps *= 2
    return before


def per_device(projected, conv_weight, conv_bias, step_size, log_decay, skip_gain):
    targets = lax.axis_size("cp")
    sections = lax.axis_size("sec")
    rows = projected.shape[0]
    width_all = projected.shape[1]
    devices = targets * sections
    groups = G // HALVES
    width_half = groups * GROUP_WIDTH
    width_here = width_half // targets
    group_targets = GROUP_WIDTH // width_here

    rim = lax.ppermute(
        projected[rows - (KERNEL - 1) :],
        ("sec", "cp"),
        [(source, source + 1) for source in range(devices - 1)],
    )
    bias = conv_bias.reshape(1, width_all)
    skip_wide = jnp.repeat(skip_gain, P_SIZE).reshape(1, WIDTH_X)
    params = pltpu.CompilerParams(vmem_limit_bytes=16 * 2**20)
    b_first = WIDTH_X // N
    c_first = b_first + G

    def columns_spec(height, width, first=0):
        return pl.BlockSpec((height, width), lambda g: (0, first + g))

    per_token = pl.BlockSpec((rows, HEAD_COUNT), lambda g: (0, 0))
    states_spec = pl.BlockSpec((group_targets, N + 8, width_here), lambda g: (g, 0, 0))
    entering_spec = pl.BlockSpec((group_targets, N, width_here), lambda g: (g, 0, 0))

    def conv_states(half):
        first = half * groups

        def three(height):
            return [
                columns_spec(height, GROUP_WIDTH, first),
                columns_spec(height, N, b_first + first),
                columns_spec(height, N, c_first + first),
            ]

        return pl.pallas_call(
            functools.partial(conv_states_kernel, first),
            grid=(groups,),
            in_specs=three(rows) + three(KERNEL - 1) + three(KERNEL) + three(1) + [per_token] * 2,
            out_specs=[
                columns_spec(rows, GROUP_WIDTH),
                columns_spec(rows, N),
                columns_spec(rows, N),
                states_spec,
            ],
            out_shape=[
                jax.ShapeDtypeStruct((rows, width_half), BF16),
                jax.ShapeDtypeStruct((rows, groups * N), BF16),
                jax.ShapeDtypeStruct((rows, groups * N), BF16),
                jax.ShapeDtypeStruct((targets, N + 8, width_here), BF16),
            ],
            scratch_shapes=[pltpu.VMEM((rows + 8, GROUP_WIDTH), F32)],
            compiler_params=params,
            name="conv_states",
        )(
            projected, projected, projected, rim, rim, rim, conv_weight, conv_weight, conv_weight,
            bias, bias, bias, step_size, log_decay,
        )

    def within_chunk(half, values, keys_b, query_c):
        first = half * groups
        return pl.pallas_call(
            functools.partial(within_kernel, first),
            grid=(groups,),
            in_specs=[
                columns_spec(rows, GROUP_WIDTH),
                columns_spec(rows, N),
                columns_spec(rows, N),
                per_token,
                per_token,
                columns_spec(1, GROUP_WIDTH, first),
            ],
            out_specs=columns_spec(rows, GROUP_WIDTH),
            out_shape=jax.ShapeDtypeStruct((rows, width_half), F32),
            scratch_shapes=[pltpu.VMEM((HEAD_COUNT, rows), F32)] * 2,
            compiler_params=params,
            name="within",
        )(values, keys_b, query_c, step_size, log_decay, skip_wide)

    def section_total(states):
        return pl.pallas_call(
            section_total_kernel,
            out_shape=jax.ShapeDtypeStruct((N + 8, width_here), F32),
            compiler_params=params,
            name="section_total",
        )(states)

    def entering_states(states, carried_in):
        return pl.pallas_call(
            entering_kernel,
            out_shape=jax.ShapeDtypeStruct((targets, N, width_here), BF16),
            compiler_params=params,
            name="entering",
        )(states, carried_in)

    def outputs(half, within, query_c, entering, so_far):
        first = half * groups
        carried = [] if so_far is None else [so_far]
        return pl.pallas_call(
            functools.partial(outputs_kernel, first),
            grid=(groups,),
            in_specs=[
                columns_spec(rows, GROUP_WIDTH),
                columns_spec(rows, N),
                per_token,
                entering_spec,
            ]
            + [pl.BlockSpec(memory_space=pl.ANY)] * len(carried),
            out_specs=columns_spec(rows, GROUP_WIDTH, first),
            out_shape=jax.ShapeDtypeStruct((rows, WIDTH_X), BF16),
            input_output_aliases={4: 0} if carried else {},
            compiler_params=params,
            name="outputs",
        )(within, query_c, log_decay, entering, *carried)

    def exchanged(value):
        return lax.all_to_all(value, "cp", split_axis=0, concat_axis=0, tiled=True)

    convs = [conv_states(half) for half in range(HALVES)]
    states = [exchanged(conv[3]) for conv in convs]
    withins = [within_chunk(half, *convs[half][:3]) for half in range(HALVES)]
    arrived = []
    leaving = None
    for half in range(HALVES):
        state = states[half]
        if half:
            state, leaving = lax.optimization_barrier((state, leaving))
            arrived.append(exchanged(leaving))
        leaving = entering_states(state, before_section(section_total(state), params))
    if arrived:
        arrived[-1], leaving = lax.optimization_barrier((arrived[-1], leaving))
    arrived.append(exchanged(leaving))
    result = None
    for half in range(HALVES):
        result = outputs(half, withins[half], convs[half][2], arrived[half], result)
    return result


def solution(mesh):
    in_specs = (
        P(("sec", "cp"), None),
        P(),
        P(),
        P(("sec", "cp"), None),
        P(("sec", "cp"), None),
        P(),
    )
    out_specs = P(("sec", "cp"), None)
    return jax.shard_map(
        per_device, mesh=mesh, in_specs=in_specs, out_specs=out_specs, check_vma=False
    )
```

```python
import functools

import jax
import jax.numpy as jnp
from jax import lax
from jax.experimental import pallas as pl
from jax.experimental.pallas import tpu as pltpu
from jax.sharding import PartitionSpec as P

HEAD_COUNT = 128
P_SIZE = 64
N = 128
G = 8
KERNEL = 4
GROUP_HEADS = HEAD_COUNT // G
GROUP_WIDTH = GROUP_HEADS * P_SIZE
WIDTH_X = HEAD_COUNT * P_SIZE
F32 = jnp.float32
BF16 = jnp.bfloat16
HALVES = 2
RADIX = 4


def lower_ones(rows):
    down = lax.broadcasted_iota(jnp.int32, (rows, rows), 0)
    across = lax.broadcasted_iota(jnp.int32, (rows, rows), 1)
    return down >= across


def dot(a, b, a_dim, b_dim):
    return lax.dot_general(a, b, (((a_dim,), (b_dim,)), ((), ())), preferred_element_type=F32)


def running_sum(decay):
    return dot(lower_ones(decay.shape[0]).astype(BF16), decay, 1, 0)


def group_columns(columns, group):
    heads = columns.shape[1]
    return pltpu.roll(columns, lax.rem(heads - group * GROUP_HEADS, heads), 1)[:, :GROUP_HEADS]


def over_heads(columns):
    rows = columns.shape[0]
    left = lax.broadcasted_iota(jnp.int32, (rows, 2 * P_SIZE), 1) < P_SIZE
    return jnp.concatenate(
        [
            jnp.where(left, columns[:, h : h + 1], columns[:, h + 1 : h + 2])
            for h in range(0, columns.shape[1], 2)
        ],
        axis=1,
    )


def conv_silu(columns, rim, weights, biases, pad):
    rows = columns.shape[0]
    width = columns.shape[1]
    pad[8 - (KERNEL - 1) : 8, 0:width] = rim.astype(F32)
    pad[8 : 8 + rows, 0:width] = columns.astype(F32)
    summed = biases
    for tap in range(KERNEL):
        first = 8 - (KERNEL - 1) + tap
        summed = summed + weights[tap : tap + 1, :] * pad[first : first + rows, 0:width]
    return (summed / (1.0 + jnp.exp(-summed))).astype(BF16)


def decay_rows(total):
    high = total.astype(BF16).astype(F32)
    middle = (total - high).astype(BF16).astype(F32)
    row = lax.broadcasted_iota(jnp.int32, (8, total.shape[1]), 0)
    pieces = jnp.where(row == 0, high, jnp.where(row == 1, middle, total - high - middle))
    return jnp.where(row < 3, pieces, 0.0).astype(BF16)


def decay_of(rows):
    return jnp.sum(rows.astype(F32), axis=0, keepdims=True)


def conv_states_kernel(
    first_group, x_in, b_in, c_in, x_rim, b_rim, c_rim, x_w, b_w, c_w, x_bias, b_bias, c_bias, step, decay,
    x_out, b_out, c_out, states, pad,
):
    values = conv_silu(x_in[...], x_rim[...], x_w[...], x_bias[...], pad)
    keys_b = conv_silu(b_in[...], b_rim[...], b_w[...], b_bias[...], pad)
    query_c = conv_silu(c_in[...], c_rim[...], c_w[...], c_bias[...], pad)
    x_out[...] = values
    b_out[...] = keys_b
    c_out[...] = query_c
    group = first_group + pl.program_id(0)
    rows = x_in.shape[0]
    running = group_columns(running_sum(decay[...]), group)
    steps = group_columns(step[...].astype(F32), group)
    weight = jnp.exp(running[rows - 1 : rows, :] - running) * steps
    weighted = (values.astype(F32) * over_heads(weight)).astype(BF16)
    targets, _, width = states.shape
    pieces = decay_rows(over_heads(running[rows - 1 : rows, :]))
    for target in range(targets):
        at = slice(target * width, (target + 1) * width)
        states[target, 0:N, :] = dot(keys_b, weighted[:, at], 0, 0).astype(BF16)
        states[target, N : N + 8, :] = pieces[:, at]


def within_kernel(first_group, x_in, b_in, c_in, step, decay, skip, out, running_all, steps_all):
    scores = dot(c_in[...], b_in[...], 1, 1)
    causal = lower_ones(scores.shape[0])
    @pl.when(pl.program_id(0) == 0)
    def _():
        running_all[...] = dot(decay[...], causal.astype(BF16), 0, 1)
        steps_all[...] = step[...].astype(F32).T

    group = first_group + pl.program_id(0)
    running = group_columns(running_sum(decay[...]), group)
    heads = pl.ds(pl.multiple_of(group * GROUP_HEADS, GROUP_HEADS), GROUP_HEADS)
    running_t = running_all[heads, :]
    steps = steps_all[heads, :]
    scores = jnp.where(causal, scores, 0.0)
    for pair in range(GROUP_HEADS // 2):
        parts = []
        x_pair = x_in[:, pair * 2 * P_SIZE : (pair + 1) * 2 * P_SIZE]
        for h in (2 * pair, 2 * pair + 1):
            gap = jnp.where(causal, running[:, h : h + 1] - running_t[h : h + 1, :], -jnp.inf)
            mix = (scores * jnp.exp(gap) * steps[h : h + 1, :]).astype(BF16)
            parts.append(dot(mix, x_pair[:, (h % 2) * P_SIZE : (h % 2 + 1) * P_SIZE], 1, 0))
        at = slice(pair * 2 * P_SIZE, (pair + 1) * 2 * P_SIZE)
        out[:, at] = jnp.concatenate(parts, axis=1) + skip[:, at] * x_pair.astype(F32)


def chunk_decays(states):
    return jnp.sum(states[:, N : N + 8, :].astype(F32), axis=1)


def section_total_kernel(states, total):
    chunks = states.shape[0]
    decays = chunk_decays(states)
    gains = jnp.exp(decays)
    for part in range(N // 32):
        at = slice(part * 32, (part + 1) * 32)
        carried = states[0, at, :].astype(F32)
        for chunk in range(1, chunks):
            carried = gains[chunk : chunk + 1, :] * carried + states[chunk, at, :].astype(F32)
        total[at, :] = carried.astype(BF16)
    total[N : N + 8, :] = decay_rows(jnp.sum(decays, axis=0, keepdims=True))


def chained(parts, at):
    state = parts[-1][at, :].astype(F32)
    for part in reversed(parts[:-1]):
        gain = jnp.exp(decay_of(part[N : N + 8, :]))
        state = part[at, :].astype(F32) + gain * state
    return state


def join_kernel(own, *parts):
    *nearby, before, through = parts
    decay_own = decay_of(own[N : N + 8, :])
    decay_near = sum(decay_of(part[N : N + 8, :]) for part in nearby)
    near = chained(nearby, slice(0, N))
    before[0:N, :] = near
    before[N : N + 8, :] = jnp.broadcast_to(decay_near, (8, near.shape[1]))
    through[0:N, :] = (own[0:N, :].astype(F32) + jnp.exp(decay_own) * near).astype(BF16)
    through[N : N + 8, :] = decay_rows(decay_own + decay_near)


def entering_kernel(states, before, *parts):
    *earlier, entering = parts
    chunks = states.shape[0]
    gains = jnp.exp(chunk_decays(states))
    gain_near = jnp.exp(before[N : N + 1, :])
    for part in range(N // 32):
        at = slice(part * 32, (part + 1) * 32)
        carried = before[at, :] + gain_near * chained(earlier, at)
        for chunk in range(chunks):
            entering[chunk, at, :] = carried.astype(BF16)
            carried = gains[chunk : chunk + 1, :] * carried + states[chunk, at, :].astype(F32)


def outputs_kernel(first_group, within, c_in, decay, entering, *rest):
    out = rest[-1]
    group = first_group + pl.program_id(0)
    growth = over_heads(jnp.exp(group_columns(running_sum(decay[...]), group)))
    query_c = c_in[...]
    targets, _, width = entering.shape
    for target in range(targets):
        at = slice(target * width, (target + 1) * width)
        out[:, at] = (within[:, at] + growth[:, at] * dot(query_c, entering[target], 1, 0)).astype(
            BF16
        )


def from_earlier(value, step, count):
    sections = lax.axis_size("sec")
    return [
        lax.ppermute(value, "sec", [(source, source + by) for source in range(sections - by)])
        for by in range(step, step * count, step)
        if by < sections
    ]


def before_section(total, params):
    before, through = pl.pallas_call(
        join_kernel,
        out_shape=[
            jax.ShapeDtypeStruct(total.shape, F32),
            jax.ShapeDtypeStruct(total.shape, BF16),
        ],
        compiler_params=params,
        name="join",
    )(total, *from_earlier(total, 1, RADIX))
    return before, *from_earlier(through, RADIX, RADIX)


def per_device(projected, conv_weight, conv_bias, step_size, log_decay, skip_gain):
    targets = lax.axis_size("cp")
    sections = lax.axis_size("sec")
    assert sections <= RADIX * RADIX
    rows = projected.shape[0]
    width_all = projected.shape[1]
    devices = targets * sections
    groups = G // HALVES
    width_half = groups * GROUP_WIDTH
    width_here = width_half // targets
    group_targets = GROUP_WIDTH // width_here

    rim = lax.ppermute(
        projected[rows - (KERNEL - 1) :],
        ("sec", "cp"),
        [(source, source + 1) for source in range(devices - 1)],
    )
    bias = conv_bias.reshape(1, width_all)
    skip_wide = jnp.repeat(skip_gain, P_SIZE).reshape(1, WIDTH_X)
    params = pltpu.CompilerParams(vmem_limit_bytes=16 * 2**20)
    b_first = WIDTH_X // N
    c_first = b_first + G

    def columns_spec(height, width, first=0):
        return pl.BlockSpec((height, width), lambda g: (0, first + g))

    per_token = pl.BlockSpec((rows, HEAD_COUNT), lambda g: (0, 0))
    states_spec = pl.BlockSpec((group_targets, N + 8, width_here), lambda g: (g, 0, 0))
    entering_spec = pl.BlockSpec((group_targets, N, width_here), lambda g: (g, 0, 0))

    def conv_states(half):
        first = half * groups

        def three(height):
            return [
                columns_spec(height, GROUP_WIDTH, first),
                columns_spec(height, N, b_first + first),
                columns_spec(height, N, c_first + first),
            ]

        return pl.pallas_call(
            functools.partial(conv_states_kernel, first),
            grid=(groups,),
            in_specs=three(rows) + three(KERNEL - 1) + three(KERNEL) + three(1) + [per_token] * 2,
            out_specs=[
                columns_spec(rows, GROUP_WIDTH),
                columns_spec(rows, N),
                columns_spec(rows, N),
                states_spec,
            ],
            out_shape=[
                pltpu.HBM((rows, width_half), BF16),
                pltpu.HBM((rows, groups * N), BF16),
                pltpu.HBM((rows, groups * N), BF16),
                pltpu.HBM((targets, N + 8, width_here), BF16),
            ],
            scratch_shapes=[pltpu.VMEM((rows + 8, GROUP_WIDTH), F32)],
            compiler_params=params,
            name="conv_states",
        )(
            projected, projected, projected, rim, rim, rim, conv_weight, conv_weight, conv_weight,
            bias, bias, bias, step_size, log_decay,
        )

    def within_chunk(half, values, keys_b, query_c):
        first = half * groups
        return pl.pallas_call(
            functools.partial(within_kernel, first),
            grid=(groups,),
            in_specs=[
                columns_spec(rows, GROUP_WIDTH),
                columns_spec(rows, N),
                columns_spec(rows, N),
                per_token,
                per_token,
                columns_spec(1, GROUP_WIDTH, first),
            ],
            out_specs=columns_spec(rows, GROUP_WIDTH),
            out_shape=pltpu.HBM((rows, width_half), F32),
            scratch_shapes=[pltpu.VMEM((HEAD_COUNT, rows), F32)] * 2,
            compiler_params=params,
            name="within",
        )(values, keys_b, query_c, step_size, log_decay, skip_wide)

    def section_total(states):
        return pl.pallas_call(
            section_total_kernel,
            out_shape=jax.ShapeDtypeStruct((N + 8, width_here), BF16),
            compiler_params=params,
            name="section_total",
        )(states)

    def entering_states(states, carried_in):
        return pl.pallas_call(
            entering_kernel,
            out_shape=pltpu.HBM((targets, N, width_here), BF16),
            compiler_params=params,
            name="entering",
        )(states, *carried_in)

    def outputs(half, within, query_c, entering, so_far):
        first = half * groups
        carried = [] if so_far is None else [so_far]
        return pl.pallas_call(
            functools.partial(outputs_kernel, first),
            grid=(groups,),
            in_specs=[
                columns_spec(rows, GROUP_WIDTH),
                columns_spec(rows, N),
                per_token,
                entering_spec,
            ]
            + [pl.BlockSpec(memory_space=pl.ANY)] * len(carried),
            out_specs=columns_spec(rows, GROUP_WIDTH, first),
            out_shape=jax.ShapeDtypeStruct((rows, WIDTH_X), BF16),
            input_output_aliases={4: 0} if carried else {},
            compiler_params=params,
            name="outputs",
        )(within, query_c, log_decay, entering, *carried)

    def exchanged(value):
        swapped = lax.all_to_all(value, "cp", split_axis=0, concat_axis=0, tiled=True)
        return pltpu.with_memory_space_constraint(swapped, pltpu.HBM)

    projected, conv_weight, bias, step_size, log_decay, skip_wide = (
        pltpu.with_memory_space_constraint(value, pltpu.HBM)
        for value in (projected, conv_weight, bias, step_size, log_decay, skip_wide)
    )
    convs = [conv_states(half) for half in range(HALVES)]
    states = [exchanged(conv[3]) for conv in convs]
    withins = [within_chunk(half, *convs[half][:3]) for half in range(HALVES)]
    arrived = []
    leaving = None
    for half in range(HALVES):
        state = states[half]
        if half:
            state, leaving = lax.optimization_barrier((state, leaving))
            arrived.append(exchanged(leaving))
        leaving = entering_states(state, before_section(section_total(state), params))
    if arrived:
        arrived[-1], leaving = lax.optimization_barrier((arrived[-1], leaving))
    arrived.append(exchanged(leaving))
    result = None
    for half in range(HALVES):
        result = outputs(half, withins[half], convs[half][2], arrived[half], result)
    return result


def solution(mesh):
    in_specs = (
        P(("sec", "cp"), None),
        P(),
        P(),
        P(("sec", "cp"), None),
        P(("sec", "cp"), None),
        P(),
    )
    out_specs = P(("sec", "cp"), None)
    return jax.shard_map(
        per_device, mesh=mesh, in_specs=in_specs, out_specs=out_specs, check_vma=False
    )
```

```python
import functools

import jax
import jax.numpy as jnp
from jax import lax
from jax.experimental import pallas as pl
from jax.experimental.pallas import tpu as pltpu
from jax.sharding import PartitionSpec as P

HEAD_COUNT = 128
P_SIZE = 64
N = 128
G = 8
KERNEL = 4
GROUP_HEADS = HEAD_COUNT // G
GROUP_WIDTH = GROUP_HEADS * P_SIZE
WIDTH_X = HEAD_COUNT * P_SIZE
F32 = jnp.float32
BF16 = jnp.bfloat16
HALVES = 2
RADIX = 4
CONV_GROUPS = 4
OUTPUT_GROUPS = 4


def lower_ones(rows):
    down = lax.broadcasted_iota(jnp.int32, (rows, rows), 0)
    across = lax.broadcasted_iota(jnp.int32, (rows, rows), 1)
    return down >= across


def dot(a, b, a_dim, b_dim):
    return lax.dot_general(a, b, (((a_dim,), (b_dim,)), ((), ())), preferred_element_type=F32)


def running_sum(decay):
    return dot(lower_ones(decay.shape[0]).astype(BF16), decay, 1, 0)


def group_columns(columns, group):
    heads = columns.shape[1]
    return pltpu.roll(columns, lax.rem(heads - group * GROUP_HEADS, heads), 1)[:, :GROUP_HEADS]


def three_parts(value):
    high = value.astype(BF16).astype(F32)
    middle = (value - high).astype(BF16).astype(F32)
    return high, middle, value - high - middle


def spread_matrix():
    row = lax.broadcasted_iota(jnp.int32, (HEAD_COUNT, GROUP_WIDTH), 0)
    lane = lax.broadcasted_iota(jnp.int32, (HEAD_COUNT, GROUP_WIDTH), 1)
    head = lax.rem(row, GROUP_HEADS)
    return ((lane // P_SIZE == head) & (row < 3 * GROUP_HEADS)).astype(BF16)


def over_heads(parts, group, spread):
    rows = parts[0].shape[0]
    lane = lax.broadcasted_iota(jnp.int32, (rows, HEAD_COUNT), 1)
    picked = jnp.zeros((rows, HEAD_COUNT), F32)
    for place, part in enumerate(parts):
        by = lax.rem(HEAD_COUNT + (place - group) * GROUP_HEADS, HEAD_COUNT)
        moved = pltpu.roll(part, by, 1)
        inside = (lane >= place * GROUP_HEADS) & (lane < (place + 1) * GROUP_HEADS)
        picked = jnp.where(inside, moved, picked)
    return dot(picked.astype(BF16), spread, 1, 0)


def conv_silu(columns, rim, weights, biases):
    rows, width = columns.shape
    shape = (8 - (KERNEL - 1), width)
    extended = jnp.concatenate([jnp.zeros(shape, F32), rim.astype(F32), columns.astype(F32)], axis=0)
    before = pltpu.roll(extended, 1, 0)
    earlier = pltpu.roll(weights[1:2, :] * extended + weights[0:1, :] * before, 2, 0)
    summed = biases + (weights[3:4, :] * extended + weights[2:3, :] * before) + earlier
    summed = summed[8:, :]
    return (summed / (1.0 + jnp.exp(-summed))).astype(BF16)


def decay_rows(*totals):
    row = lax.broadcasted_iota(jnp.int32, (8, totals[0].shape[1]), 0)
    value = jnp.zeros(row.shape, F32)
    for which, total in enumerate(totals):
        for place, part in enumerate(three_parts(total)):
            value = jnp.where(row == 3 * which + place, part, value)
    return value.astype(BF16)


def decay_of(rows):
    return jnp.sum(rows.astype(F32), axis=0, keepdims=True)


def conv_states_kernel(
    first_group, x_in, b_in, c_in, x_rim, b_rim, c_rim, x_w, b_w, c_w, x_bias, b_bias, c_bias, step, decay,
    x_out, b_out, c_out, states, spread,
):
    rows = x_in.shape[0]
    groups = x_in.shape[1] // GROUP_WIDTH
    targets, height, width = states.shape
    running_all = running_sum(decay[...])
    weight_parts = three_parts(
        jnp.exp(running_all[rows - 1 : rows, :] - running_all) * step[...].astype(F32)
    )
    last_parts = three_parts(running_all[rows - 8 : rows, :])

    @pl.when(pl.program_id(0) == 0)
    def _():
        spread[...] = spread_matrix()

    for local in range(groups):
        group = first_group + pl.program_id(0) * groups + local
        wide = slice(local * GROUP_WIDTH, (local + 1) * GROUP_WIDTH)
        narrow = slice(local * N, (local + 1) * N)
        values = conv_silu(x_in[:, wide], x_rim[:, wide], x_w[:, wide], x_bias[:, wide])
        keys_b = conv_silu(b_in[:, narrow], b_rim[:, narrow], b_w[:, narrow], b_bias[:, narrow])
        query_c = conv_silu(c_in[:, narrow], c_rim[:, narrow], c_w[:, narrow], c_bias[:, narrow])
        x_out[:, wide] = values
        b_out[:, narrow] = keys_b
        c_out[:, narrow] = query_c
        weighted = (values.astype(F32) * over_heads(weight_parts, group, spread[...])).astype(BF16)
        summed = dot(keys_b, weighted, 0, 0).astype(BF16)
        here = range(targets // groups)
        for at in here:
            lanes = slice(at * width, (at + 1) * width)
            states[local * len(here) + at, 0:N, :] = summed[:, lanes]
        if height > N:
            pieces = decay_rows(
                *(
                    over_heads(last_parts, group + half * (G // HALVES), spread[...])[7:8, :]
                    for half in range(HALVES)
                )
            )
            for at in here:
                lanes = slice(at * width, (at + 1) * width)
                states[local * len(here) + at, N:height, :] = pieces[:, lanes]


def within_kernel(first_group, x_in, b_in, c_in, step, decay, skip, out, running_all, steps_all):
    scores = dot(c_in[...], b_in[...], 1, 1)
    causal = lower_ones(scores.shape[0])
    @pl.when(pl.program_id(0) == 0)
    def _():
        running_all[...] = dot(decay[...], causal.astype(BF16), 0, 1)
        steps_all[...] = step[...].astype(F32).T

    group = first_group + pl.program_id(0)
    running = group_columns(running_sum(decay[...]), group)
    heads = pl.ds(pl.multiple_of(group * GROUP_HEADS, GROUP_HEADS), GROUP_HEADS)
    running_t = running_all[heads, :]
    steps = steps_all[heads, :]
    scores = jnp.where(causal, scores, 0.0)
    for pair in range(GROUP_HEADS // 2):
        parts = []
        x_pair = x_in[:, pair * 2 * P_SIZE : (pair + 1) * 2 * P_SIZE]
        for h in (2 * pair, 2 * pair + 1):
            gap = jnp.where(causal, running[:, h : h + 1] - running_t[h : h + 1, :], -jnp.inf)
            mix = (scores * jnp.exp(gap) * steps[h : h + 1, :]).astype(BF16)
            parts.append(dot(mix, x_pair[:, (h % 2) * P_SIZE : (h % 2 + 1) * P_SIZE], 1, 0))
        at = slice(pair * 2 * P_SIZE, (pair + 1) * 2 * P_SIZE)
        out[:, at] = jnp.concatenate(parts, axis=1) + skip[:, at] * x_pair.astype(F32)


def chunk_decays(decays, half):
    return jnp.sum(decays[:, 3 * half : 3 * half + 3, :].astype(F32), axis=1)


def section_total_kernel(half, states, decays, total):
    chunks = states.shape[0]
    sums = chunk_decays(decays, half)
    gains = jnp.exp(sums)
    for part in range(N // 32):
        at = slice(part * 32, (part + 1) * 32)
        carried = states[0, at, :].astype(F32)
        for chunk in range(1, chunks):
            carried = gains[chunk : chunk + 1, :] * carried + states[chunk, at, :].astype(F32)
        total[at, :] = carried.astype(BF16)
    total[N : N + 8, :] = decay_rows(jnp.sum(sums, axis=0, keepdims=True))


def chained(parts, at):
    state = parts[-1][at, :].astype(F32)
    for part in reversed(parts[:-1]):
        gain = jnp.exp(decay_of(part[N : N + 8, :]))
        state = part[at, :].astype(F32) + gain * state
    return state


def join_kernel(own, *parts):
    *nearby, before, through = parts
    decay_own = decay_of(own[N : N + 8, :])
    decay_near = sum(decay_of(part[N : N + 8, :]) for part in nearby)
    near = chained(nearby, slice(0, N))
    before[0:N, :] = near
    before[N : N + 8, :] = jnp.broadcast_to(decay_near, (8, near.shape[1]))
    through[0:N, :] = (own[0:N, :].astype(F32) + jnp.exp(decay_own) * near).astype(BF16)
    through[N : N + 8, :] = decay_rows(decay_own + decay_near)


def entering_kernel(half, states, decays, before, *parts):
    *earlier, entering = parts
    chunks = states.shape[0]
    gains = jnp.exp(chunk_decays(decays, half))
    gain_near = jnp.exp(before[N : N + 1, :])
    for part in range(N // 32):
        at = slice(part * 32, (part + 1) * 32)
        carried = before[at, :] + gain_near * chained(earlier, at)
        for chunk in range(chunks):
            entering[chunk, at, :] = carried.astype(BF16)
            carried = gains[chunk : chunk + 1, :] * carried + states[chunk, at, :].astype(F32)


def outputs_kernel(first_group, within, c_in, decay, entering, *rest):
    out, spread = rest[-2:]
    groups = out.shape[1] // GROUP_WIDTH
    targets, _, width = entering.shape
    growth_parts = three_parts(jnp.exp(running_sum(decay[...])))

    @pl.when(pl.program_id(0) == 0)
    def _():
        spread[...] = spread_matrix()

    for local in range(groups):
        group = first_group + pl.program_id(0) * groups + local
        growth = over_heads(growth_parts, group, spread[...])
        query_c = c_in[:, local * N : (local + 1) * N]
        for at in range(targets // groups):
            lanes = slice(at * width, (at + 1) * width)
            wide = slice(local * GROUP_WIDTH + at * width, local * GROUP_WIDTH + (at + 1) * width)
            carried = dot(query_c, entering[local * (targets // groups) + at], 1, 0)
            out[:, wide] = (within[:, wide] + growth[:, lanes] * carried).astype(BF16)


def from_earlier(value, step, count):
    sections = lax.axis_size("sec")
    return [
        lax.ppermute(value, "sec", [(source, source + by) for source in range(sections - by)])
        for by in range(step, step * count, step)
        if by < sections
    ]


def before_section(total, params):
    before, through = pl.pallas_call(
        join_kernel,
        out_shape=[
            jax.ShapeDtypeStruct(total.shape, F32),
            jax.ShapeDtypeStruct(total.shape, BF16),
        ],
        compiler_params=params,
        name="join",
    )(total, *from_earlier(total, 1, RADIX))
    return before, *from_earlier(through, RADIX, RADIX)


def per_device(projected, conv_weight, conv_bias, step_size, log_decay, skip_gain):
    targets = lax.axis_size("cp")
    sections = lax.axis_size("sec")
    assert sections <= RADIX * RADIX
    rows = projected.shape[0]
    width_all = projected.shape[1]
    devices = targets * sections
    groups = G // HALVES
    width_half = groups * GROUP_WIDTH
    width_here = width_half // targets
    group_targets = GROUP_WIDTH // width_here

    rim = lax.ppermute(
        projected[rows - (KERNEL - 1) :],
        ("sec", "cp"),
        [(source, source + 1) for source in range(devices - 1)],
    )
    bias = conv_bias.reshape(1, width_all)
    skip_wide = jnp.repeat(skip_gain, P_SIZE).reshape(1, WIDTH_X)
    params = pltpu.CompilerParams(vmem_limit_bytes=16 * 2**20)
    b_first = WIDTH_X // N
    c_first = b_first + G

    def columns_spec(height, width, first=0):
        return pl.BlockSpec((height, width), lambda g: (0, first + g))

    per_token = pl.BlockSpec((rows, HEAD_COUNT), lambda g: (0, 0))
    def conv_states(half):
        at_once = CONV_GROUPS
        first = half * groups // at_once
        wide = at_once * GROUP_WIDTH
        narrow = at_once * N
        state_rows = N if half else N + 8

        def three(height):
            return [
                columns_spec(height, wide, first),
                columns_spec(height, narrow, b_first // at_once + first),
                columns_spec(height, narrow, c_first // at_once + first),
            ]

        return pl.pallas_call(
            functools.partial(conv_states_kernel, half * groups),
            grid=(groups // at_once,),
            in_specs=three(rows) + three(KERNEL - 1) + three(KERNEL) + three(1) + [per_token] * 2,
            out_specs=[
                columns_spec(rows, wide),
                columns_spec(rows, narrow),
                columns_spec(rows, narrow),
                pl.BlockSpec(
                    (at_once * group_targets, state_rows, width_here), lambda g: (g, 0, 0)
                ),
            ],
            out_shape=[
                pltpu.HBM((rows, width_half), BF16),
                pltpu.HBM((rows, groups * N), BF16),
                pltpu.HBM((rows, groups * N), BF16),
                pltpu.HBM((targets, state_rows, width_here), BF16),
            ],
            scratch_shapes=[pltpu.VMEM((HEAD_COUNT, GROUP_WIDTH), BF16)],
            compiler_params=params,
            name="conv_states",
        )(
            projected, projected, projected, rim, rim, rim, conv_weight, conv_weight, conv_weight,
            bias, bias, bias, step_size, log_decay,
        )

    def within_chunk(half, values, keys_b, query_c):
        first = half * groups
        return pl.pallas_call(
            functools.partial(within_kernel, first),
            grid=(groups,),
            in_specs=[
                columns_spec(rows, GROUP_WIDTH),
                columns_spec(rows, N),
                columns_spec(rows, N),
                per_token,
                per_token,
                columns_spec(1, GROUP_WIDTH, first),
            ],
            out_specs=columns_spec(rows, GROUP_WIDTH),
            out_shape=pltpu.HBM((rows, width_half), F32),
            scratch_shapes=[pltpu.VMEM((HEAD_COUNT, rows), F32)] * 2,
            compiler_params=params,
            name="within",
        )(values, keys_b, query_c, step_size, log_decay, skip_wide)

    arrived_specs = [
        pl.BlockSpec((targets, N, width_here), lambda g: (0, 0, 0)),
        pl.BlockSpec((targets, 8, width_here), lambda g: (0, N // 8, 0)),
    ]
    total_spec = pl.BlockSpec((N + 8, width_here), lambda g: (0, 0))

    def section_total(half, states, first_states):
        return pl.pallas_call(
            functools.partial(section_total_kernel, half),
            grid=(1,),
            in_specs=arrived_specs,
            out_specs=total_spec,
            out_shape=jax.ShapeDtypeStruct((N + 8, width_here), BF16),
            compiler_params=params,
            name="section_total",
        )(states, first_states)

    def entering_states(half, states, first_states, carried_in):
        return pl.pallas_call(
            functools.partial(entering_kernel, half),
            grid=(1,),
            in_specs=arrived_specs + [total_spec] * len(carried_in),
            out_specs=pl.BlockSpec((targets, N, width_here), lambda g: (0, 0, 0)),
            out_shape=pltpu.HBM((targets, N, width_here), BF16),
            compiler_params=params,
            name="entering",
        )(states, first_states, *carried_in)

    def outputs(half, within, query_c, entering, so_far):
        at_once = OUTPUT_GROUPS
        wide = at_once * GROUP_WIDTH
        carried = [] if so_far is None else [so_far]
        return pl.pallas_call(
            functools.partial(outputs_kernel, half * groups),
            grid=(groups // at_once,),
            in_specs=[
                columns_spec(rows, wide),
                columns_spec(rows, at_once * N),
                per_token,
                pl.BlockSpec((at_once * group_targets, N, width_here), lambda g: (g, 0, 0)),
            ]
            + [pl.BlockSpec(memory_space=pl.ANY)] * len(carried),
            out_specs=columns_spec(rows, wide, half * groups // at_once),
            out_shape=jax.ShapeDtypeStruct((rows, WIDTH_X), BF16),
            input_output_aliases={4: 0} if carried else {},
            scratch_shapes=[pltpu.VMEM((HEAD_COUNT, GROUP_WIDTH), BF16)],
            compiler_params=params,
            name="outputs",
        )(within, query_c, log_decay, entering, *carried)

    def exchanged(value):
        return lax.all_to_all(value, "cp", split_axis=0, concat_axis=0, tiled=True)

    projected, conv_weight, bias, step_size, log_decay, skip_wide = (
        pltpu.with_memory_space_constraint(value, pltpu.HBM)
        for value in (projected, conv_weight, bias, step_size, log_decay, skip_wide)
    )
    convs = [conv_states(half) for half in range(HALVES)]
    states = [exchanged(conv[3]) for conv in convs]
    withins = [within_chunk(half, *convs[half][:3]) for half in range(HALVES)]
    arrived = []
    leaving = None
    for half in range(HALVES):
        state = states[half]
        if half:
            state, leaving = lax.optimization_barrier((state, leaving))
            arrived.append(exchanged(leaving))
        total = section_total(half, state, states[0])
        leaving = entering_states(half, state, states[0], before_section(total, params))
    if arrived:
        arrived[-1], leaving = lax.optimization_barrier((arrived[-1], leaving))
    arrived.append(exchanged(leaving))
    result = None
    for half in range(HALVES):
        result = outputs(half, withins[half], convs[half][2], arrived[half], result)
    return result


def solution(mesh):
    in_specs = (
        P(("sec", "cp"), None),
        P(),
        P(),
        P(("sec", "cp"), None),
        P(("sec", "cp"), None),
        P(),
    )
    out_specs = P(("sec", "cp"), None)
    return jax.shard_map(
        per_device, mesh=mesh, in_specs=in_specs, out_specs=out_specs, check_vma=False
    )
```

```python
import functools

import jax
import jax.numpy as jnp
from jax import lax
from jax.experimental import pallas as pl
from jax.experimental.pallas import tpu as pltpu
from jax.sharding import PartitionSpec as P

HEAD_COUNT = 128
P_SIZE = 64
N = 128
G = 8
KERNEL = 4
GROUP_HEADS = HEAD_COUNT // G
GROUP_WIDTH = GROUP_HEADS * P_SIZE
WIDTH_X = HEAD_COUNT * P_SIZE
F32 = jnp.float32
BF16 = jnp.bfloat16
HALVES = 2
CONV_GROUPS = 4
OUTPUT_GROUPS = 4


def lower_ones(rows):
    down = lax.broadcasted_iota(jnp.int32, (rows, rows), 0)
    across = lax.broadcasted_iota(jnp.int32, (rows, rows), 1)
    return down >= across


def dot(a, b, a_dim, b_dim):
    return lax.dot_general(a, b, (((a_dim,), (b_dim,)), ((), ())), preferred_element_type=F32)


def running_sum(decay):
    return dot(lower_ones(decay.shape[0]).astype(BF16), decay, 1, 0)


def group_columns(columns, group):
    heads = columns.shape[1]
    return pltpu.roll(columns, lax.rem(heads - group * GROUP_HEADS, heads), 1)[:, :GROUP_HEADS]


def three_parts(value):
    high = value.astype(BF16).astype(F32)
    middle = (value - high).astype(BF16).astype(F32)
    return high, middle, value - high - middle


def spread_matrix():
    row = lax.broadcasted_iota(jnp.int32, (HEAD_COUNT, GROUP_WIDTH), 0)
    lane = lax.broadcasted_iota(jnp.int32, (HEAD_COUNT, GROUP_WIDTH), 1)
    head = lax.rem(row, GROUP_HEADS)
    return ((lane // P_SIZE == head) & (row < 3 * GROUP_HEADS)).astype(BF16)


def over_heads(parts, group, spread):
    rows = parts[0].shape[0]
    lane = lax.broadcasted_iota(jnp.int32, (rows, HEAD_COUNT), 1)
    picked = jnp.zeros((rows, HEAD_COUNT), F32)
    for place, part in enumerate(parts):
        by = lax.rem(HEAD_COUNT + (place - group) * GROUP_HEADS, HEAD_COUNT)
        moved = pltpu.roll(part, by, 1)
        inside = (lane >= place * GROUP_HEADS) & (lane < (place + 1) * GROUP_HEADS)
        picked = jnp.where(inside, moved, picked)
    return dot(picked.astype(BF16), spread, 1, 0)


def conv_silu(columns, rim, weights, biases):
    rows, width = columns.shape
    shape = (8 - (KERNEL - 1), width)
    extended = jnp.concatenate([jnp.zeros(shape, F32), rim.astype(F32), columns.astype(F32)], axis=0)
    before = pltpu.roll(extended, 1, 0)
    earlier = pltpu.roll(weights[1:2, :] * extended + weights[0:1, :] * before, 2, 0)
    summed = biases + (weights[3:4, :] * extended + weights[2:3, :] * before) + earlier
    summed = summed[8:, :]
    return (summed / (1.0 + jnp.exp(-summed))).astype(BF16)


def decay_rows(*totals):
    row = lax.broadcasted_iota(jnp.int32, (8, totals[0].shape[1]), 0)
    value = jnp.zeros(row.shape, F32)
    for which, total in enumerate(totals):
        for place, part in enumerate(three_parts(total)):
            value = jnp.where(row == 3 * which + place, part, value)
    return value.astype(BF16)


def decay_of(rows):
    return jnp.sum(rows.astype(F32), axis=0, keepdims=True)


def conv_states_kernel(
    first_group, x_in, b_in, c_in, x_rim, b_rim, c_rim, x_w, b_w, c_w, x_bias, b_bias, c_bias, step, decay,
    x_out, b_out, c_out, states, spread,
):
    rows = x_in.shape[0]
    groups = x_in.shape[1] // GROUP_WIDTH
    targets, height, width = states.shape
    running_all = running_sum(decay[...])
    weight_parts = three_parts(
        jnp.exp(running_all[rows - 1 : rows, :] - running_all) * step[...].astype(F32)
    )
    last_parts = three_parts(running_all[rows - 8 : rows, :])

    @pl.when(pl.program_id(0) == 0)
    def _():
        spread[...] = spread_matrix()

    for local in range(groups):
        group = first_group + pl.program_id(0) * groups + local
        wide = slice(local * GROUP_WIDTH, (local + 1) * GROUP_WIDTH)
        narrow = slice(local * N, (local + 1) * N)
        values = conv_silu(x_in[:, wide], x_rim[:, wide], x_w[:, wide], x_bias[:, wide])
        keys_b = conv_silu(b_in[:, narrow], b_rim[:, narrow], b_w[:, narrow], b_bias[:, narrow])
        query_c = conv_silu(c_in[:, narrow], c_rim[:, narrow], c_w[:, narrow], c_bias[:, narrow])
        x_out[:, wide] = values
        b_out[:, narrow] = keys_b
        c_out[:, narrow] = query_c
        weighted = (values.astype(F32) * over_heads(weight_parts, group, spread[...])).astype(BF16)
        summed = dot(keys_b, weighted, 0, 0).astype(BF16)
        here = range(targets // groups)
        for at in here:
            lanes = slice(at * width, (at + 1) * width)
            states[local * len(here) + at, 0:N, :] = summed[:, lanes]
        if height > N:
            pieces = decay_rows(
                *(
                    over_heads(last_parts, group + half * (G // HALVES), spread[...])[7:8, :]
                    for half in range(HALVES)
                )
            )
            for at in here:
                lanes = slice(at * width, (at + 1) * width)
                states[local * len(here) + at, N:height, :] = pieces[:, lanes]


def within_kernel(first_group, x_in, b_in, c_in, step, decay, skip, out, running_all, steps_all):
    scores = dot(c_in[...], b_in[...], 1, 1)
    causal = lower_ones(scores.shape[0])
    @pl.when(pl.program_id(0) == 0)
    def _():
        running_all[...] = dot(decay[...], causal.astype(BF16), 0, 1)
        steps_all[...] = step[...].astype(F32).T

    group = first_group + pl.program_id(0)
    running = group_columns(running_sum(decay[...]), group)
    heads = pl.ds(pl.multiple_of(group * GROUP_HEADS, GROUP_HEADS), GROUP_HEADS)
    running_t = running_all[heads, :]
    steps = steps_all[heads, :]
    scores = jnp.where(causal, scores, 0.0)
    for pair in range(GROUP_HEADS // 2):
        parts = []
        x_pair = x_in[:, pair * 2 * P_SIZE : (pair + 1) * 2 * P_SIZE]
        for h in (2 * pair, 2 * pair + 1):
            gap = jnp.where(causal, running[:, h : h + 1] - running_t[h : h + 1, :], -jnp.inf)
            mix = (scores * jnp.exp(gap) * steps[h : h + 1, :]).astype(BF16)
            parts.append(dot(mix, x_pair[:, (h % 2) * P_SIZE : (h % 2 + 1) * P_SIZE], 1, 0))
        at = slice(pair * 2 * P_SIZE, (pair + 1) * 2 * P_SIZE)
        out[:, at] = jnp.concatenate(parts, axis=1) + skip[:, at] * x_pair.astype(F32)


def chunk_decays(decays, half):
    return jnp.sum(decays[:, 3 * half : 3 * half + 3, :].astype(F32), axis=1)


def section_total_kernel(half, states, decays, total):
    chunks = states.shape[0]
    sums = chunk_decays(decays, half)
    gains = jnp.exp(sums)
    for part in range(N // 32):
        at = slice(part * 32, (part + 1) * 32)
        carried = states[0, at, :].astype(F32)
        for chunk in range(1, chunks):
            carried = gains[chunk : chunk + 1, :] * carried + states[chunk, at, :].astype(F32)
        total[at, :] = carried.astype(BF16)
    total[N : N + 8, :] = decay_rows(jnp.sum(sums, axis=0, keepdims=True))


def entering_kernel(half, states, decays, totals, entering):
    chunks = states.shape[0]
    sections = totals.shape[0]
    here = lax.axis_index("sec")
    gains = jnp.exp(chunk_decays(decays, half))
    section_gains = jnp.exp(chunk_decays(totals[:, N : N + 8, :], 0))
    for part in range(N // 32):
        at = slice(part * 32, (part + 1) * 32)
        carried = jnp.zeros((32, states.shape[2]), F32)
        for section in range(sections - 1):
            after = section_gains[section : section + 1, :] * carried
            after = after + totals[section, at, :].astype(F32)
            carried = jnp.where(section < here, after, carried)
        for chunk in range(chunks):
            entering[chunk, at, :] = carried.astype(BF16)
            carried = gains[chunk : chunk + 1, :] * carried + states[chunk, at, :].astype(F32)


def outputs_kernel(first_group, within, c_in, decay, entering, *rest):
    out, spread = rest[-2:]
    groups = out.shape[1] // GROUP_WIDTH
    targets, _, width = entering.shape
    growth_parts = three_parts(jnp.exp(running_sum(decay[...])))

    @pl.when(pl.program_id(0) == 0)
    def _():
        spread[...] = spread_matrix()

    for local in range(groups):
        group = first_group + pl.program_id(0) * groups + local
        growth = over_heads(growth_parts, group, spread[...])
        query_c = c_in[:, local * N : (local + 1) * N]
        for at in range(targets // groups):
            lanes = slice(at * width, (at + 1) * width)
            wide = slice(local * GROUP_WIDTH + at * width, local * GROUP_WIDTH + (at + 1) * width)
            carried = dot(query_c, entering[local * (targets // groups) + at], 1, 0)
            out[:, wide] = (within[:, wide] + growth[:, lanes] * carried).astype(BF16)


def per_device(projected, conv_weight, conv_bias, step_size, log_decay, skip_gain):
    targets = lax.axis_size("cp")
    sections = lax.axis_size("sec")
    rows = projected.shape[0]
    width_all = projected.shape[1]
    devices = targets * sections
    groups = G // HALVES
    width_half = groups * GROUP_WIDTH
    width_here = width_half // targets
    group_targets = GROUP_WIDTH // width_here

    rim = lax.ppermute(
        projected[rows - (KERNEL - 1) :],
        ("sec", "cp"),
        [(source, source + 1) for source in range(devices - 1)],
    )
    bias = conv_bias.reshape(1, width_all)
    skip_wide = jnp.repeat(skip_gain, P_SIZE).reshape(1, WIDTH_X)
    params = pltpu.CompilerParams(vmem_limit_bytes=16 * 2**20)
    b_first = WIDTH_X // N
    c_first = b_first + G

    def columns_spec(height, width, first=0):
        return pl.BlockSpec((height, width), lambda g: (0, first + g))

    per_token = pl.BlockSpec((rows, HEAD_COUNT), lambda g: (0, 0))
    def conv_states(half):
        at_once = CONV_GROUPS
        first = half * groups // at_once
        wide = at_once * GROUP_WIDTH
        narrow = at_once * N
        state_rows = N if half else N + 8

        def three(height):
            return [
                columns_spec(height, wide, first),
                columns_spec(height, narrow, b_first // at_once + first),
                columns_spec(height, narrow, c_first // at_once + first),
            ]

        return pl.pallas_call(
            functools.partial(conv_states_kernel, half * groups),
            grid=(groups // at_once,),
            in_specs=three(rows) + three(KERNEL - 1) + three(KERNEL) + three(1) + [per_token] * 2,
            out_specs=[
                columns_spec(rows, wide),
                columns_spec(rows, narrow),
                columns_spec(rows, narrow),
                pl.BlockSpec(
                    (at_once * group_targets, state_rows, width_here), lambda g: (g, 0, 0)
                ),
            ],
            out_shape=[
                pltpu.HBM((rows, width_half), BF16),
                pltpu.HBM((rows, groups * N), BF16),
                pltpu.HBM((rows, groups * N), BF16),
                pltpu.HBM((targets, state_rows, width_here), BF16),
            ],
            scratch_shapes=[pltpu.VMEM((HEAD_COUNT, GROUP_WIDTH), BF16)],
            compiler_params=params,
            name="conv_states",
        )(
            projected, projected, projected, rim, rim, rim, conv_weight, conv_weight, conv_weight,
            bias, bias, bias, step_size, log_decay,
        )

    def within_chunk(half, values, keys_b, query_c):
        first = half * groups
        return pl.pallas_call(
            functools.partial(within_kernel, first),
            grid=(groups,),
            in_specs=[
                columns_spec(rows, GROUP_WIDTH),
                columns_spec(rows, N),
                columns_spec(rows, N),
                per_token,
                per_token,
                columns_spec(1, GROUP_WIDTH, first),
            ],
            out_specs=columns_spec(rows, GROUP_WIDTH),
            out_shape=pltpu.HBM((rows, width_half), F32),
            scratch_shapes=[pltpu.VMEM((HEAD_COUNT, rows), F32)] * 2,
            compiler_params=params,
            name="within",
        )(values, keys_b, query_c, step_size, log_decay, skip_wide)

    arrived_specs = [
        pl.BlockSpec((targets, N, width_here), lambda g: (0, 0, 0)),
        pl.BlockSpec((targets, 8, width_here), lambda g: (0, N // 8, 0)),
    ]
    total_spec = pl.BlockSpec((N + 8, width_here), lambda g: (0, 0))

    def section_total(half, states, first_states):
        return pl.pallas_call(
            functools.partial(section_total_kernel, half),
            grid=(1,),
            in_specs=arrived_specs,
            out_specs=total_spec,
            out_shape=jax.ShapeDtypeStruct((N + 8, width_here), BF16),
            compiler_params=params,
            name="section_total",
        )(states, first_states)

    def entering_states(half, states, first_states, totals):
        return pl.pallas_call(
            functools.partial(entering_kernel, half),
            grid=(1,),
            in_specs=arrived_specs
            + [pl.BlockSpec((sections, N + 8, width_here), lambda g: (0, 0, 0))],
            out_specs=pl.BlockSpec((targets, N, width_here), lambda g: (0, 0, 0)),
            out_shape=pltpu.HBM((targets, N, width_here), BF16),
            compiler_params=params,
            name="entering",
        )(states, first_states, totals)

    def outputs(half, within, query_c, entering, so_far):
        at_once = OUTPUT_GROUPS
        wide = at_once * GROUP_WIDTH
        carried = [] if so_far is None else [so_far]
        return pl.pallas_call(
            functools.partial(outputs_kernel, half * groups),
            grid=(groups // at_once,),
            in_specs=[
                columns_spec(rows, wide),
                columns_spec(rows, at_once * N),
                per_token,
                pl.BlockSpec((at_once * group_targets, N, width_here), lambda g: (g, 0, 0)),
            ]
            + [pl.BlockSpec(memory_space=pl.ANY)] * len(carried),
            out_specs=columns_spec(rows, wide, half * groups // at_once),
            out_shape=jax.ShapeDtypeStruct((rows, WIDTH_X), BF16),
            input_output_aliases={4: 0} if carried else {},
            scratch_shapes=[pltpu.VMEM((HEAD_COUNT, GROUP_WIDTH), BF16)],
            compiler_params=params,
            name="outputs",
        )(within, query_c, log_decay, entering, *carried)

    def exchanged(value):
        return lax.all_to_all(value, "cp", split_axis=0, concat_axis=0, tiled=True)

    projected, conv_weight, bias, step_size, log_decay, skip_wide = (
        pltpu.with_memory_space_constraint(value, pltpu.HBM)
        for value in (projected, conv_weight, bias, step_size, log_decay, skip_wide)
    )
    convs = [conv_states(half) for half in range(HALVES)]
    states = [exchanged(conv[3]) for conv in convs]
    withins = [within_chunk(half, *convs[half][:3]) for half in range(HALVES)]
    arrived = []
    leaving = None
    for half in range(HALVES):
        state = states[half]
        if half:
            state, leaving = lax.optimization_barrier((state, leaving))
            arrived.append(exchanged(leaving))
        totals = lax.all_gather(section_total(half, state, states[0]), "sec")
        leaving = entering_states(half, state, states[0], totals)
    if arrived:
        arrived[-1], leaving = lax.optimization_barrier((arrived[-1], leaving))
    arrived.append(exchanged(leaving))
    result = None
    for half in range(HALVES):
        result = outputs(half, withins[half], convs[half][2], arrived[half], result)
    return result


def solution(mesh):
    in_specs = (
        P(("sec", "cp"), None),
        P(),
        P(),
        P(("sec", "cp"), None),
        P(("sec", "cp"), None),
        P(),
    )
    out_specs = P(("sec", "cp"), None)
    return jax.shard_map(
        per_device, mesh=mesh, in_specs=in_specs, out_specs=out_specs, check_vma=False
    )
```

```python
import functools

import jax
import jax.numpy as jnp
from jax import lax
from jax.experimental import pallas as pl
from jax.experimental.pallas import tpu as pltpu
from jax.sharding import PartitionSpec as P

HEAD_COUNT = 128
P_SIZE = 64
N = 128
G = 8
KERNEL = 4
GROUP_HEADS = HEAD_COUNT // G
GROUP_WIDTH = GROUP_HEADS * P_SIZE
WIDTH_X = HEAD_COUNT * P_SIZE
F32 = jnp.float32
BF16 = jnp.bfloat16
HALVES = 2
CONV_GROUPS = 4
OUTPUT_GROUPS = 4


def lower_ones(rows):
    down = lax.broadcasted_iota(jnp.int32, (rows, rows), 0)
    across = lax.broadcasted_iota(jnp.int32, (rows, rows), 1)
    return down >= across


def dot(a, b, a_dim, b_dim):
    return lax.dot_general(a, b, (((a_dim,), (b_dim,)), ((), ())), preferred_element_type=F32)


def running_sum(decay):
    return dot(lower_ones(decay.shape[0]).astype(BF16), decay, 1, 0)


def group_columns(columns, group):
    heads = columns.shape[1]
    return pltpu.roll(columns, lax.rem(heads - group * GROUP_HEADS, heads), 1)[:, :GROUP_HEADS]


def three_parts(value):
    high = value.astype(BF16).astype(F32)
    middle = (value - high).astype(BF16).astype(F32)
    return high, middle, value - high - middle


def spread_matrix():
    row = lax.broadcasted_iota(jnp.int32, (HEAD_COUNT, GROUP_WIDTH), 0)
    lane = lax.broadcasted_iota(jnp.int32, (HEAD_COUNT, GROUP_WIDTH), 1)
    head = lax.rem(row, GROUP_HEADS)
    return ((lane // P_SIZE == head) & (row < 3 * GROUP_HEADS)).astype(BF16)


def over_heads(parts, group, spread):
    rows = parts[0].shape[0]
    lane = lax.broadcasted_iota(jnp.int32, (rows, HEAD_COUNT), 1)
    picked = jnp.zeros((rows, HEAD_COUNT), F32)
    for place, part in enumerate(parts):
        by = lax.rem(HEAD_COUNT + (place - group) * GROUP_HEADS, HEAD_COUNT)
        moved = pltpu.roll(part, by, 1)
        inside = (lane >= place * GROUP_HEADS) & (lane < (place + 1) * GROUP_HEADS)
        picked = jnp.where(inside, moved, picked)
    return dot(picked.astype(BF16), spread, 1, 0)


def conv_silu(columns, rim, weights, biases):
    rows, width = columns.shape
    shape = (8 - (KERNEL - 1), width)
    extended = jnp.concatenate([jnp.zeros(shape, F32), rim.astype(F32), columns.astype(F32)], axis=0)
    before = pltpu.roll(extended, 1, 0)
    earlier = pltpu.roll(weights[1:2, :] * extended + weights[0:1, :] * before, 2, 0)
    summed = biases + (weights[3:4, :] * extended + weights[2:3, :] * before) + earlier
    summed = summed[8:, :]
    return (summed / (1.0 + jnp.exp(-summed))).astype(BF16)


def decay_rows(*totals):
    row = lax.broadcasted_iota(jnp.int32, (8, totals[0].shape[1]), 0)
    value = jnp.zeros(row.shape, F32)
    for which, total in enumerate(totals):
        for place, part in enumerate(three_parts(total)):
            value = jnp.where(row == 3 * which + place, part, value)
    return value.astype(BF16)


def decay_of(rows):
    return jnp.sum(rows.astype(F32), axis=0, keepdims=True)


def conv_states_kernel(
    first_group, x_in, b_in, c_in, x_rim, b_rim, c_rim, x_w, b_w, c_w, x_bias, b_bias, c_bias, step, decay,
    x_out, b_out, c_out, states, spread,
):
    rows = x_in.shape[0]
    groups = x_in.shape[1] // GROUP_WIDTH
    targets, height, width = states.shape
    running_all = running_sum(decay[...])
    weight_parts = three_parts(
        jnp.exp(running_all[rows - 1 : rows, :] - running_all) * step[...].astype(F32)
    )
    last_parts = three_parts(running_all[rows - 8 : rows, :])

    @pl.when(pl.program_id(0) == 0)
    def _():
        spread[...] = spread_matrix()

    for local in range(groups):
        group = first_group + pl.program_id(0) * groups + local
        wide = slice(local * GROUP_WIDTH, (local + 1) * GROUP_WIDTH)
        narrow = slice(local * N, (local + 1) * N)
        values = conv_silu(x_in[:, wide], x_rim[:, wide], x_w[:, wide], x_bias[:, wide])
        keys_b = conv_silu(b_in[:, narrow], b_rim[:, narrow], b_w[:, narrow], b_bias[:, narrow])
        query_c = conv_silu(c_in[:, narrow], c_rim[:, narrow], c_w[:, narrow], c_bias[:, narrow])
        x_out[:, wide] = values
        b_out[:, narrow] = keys_b
        c_out[:, narrow] = query_c
        weighted = (values.astype(F32) * over_heads(weight_parts, group, spread[...])).astype(BF16)
        summed = dot(keys_b, weighted, 0, 0).astype(BF16)
        here = range(targets // groups)
        for at in here:
            lanes = slice(at * width, (at + 1) * width)
            states[local * len(here) + at, 0:N, :] = summed[:, lanes]
        if height > N:
            pieces = decay_rows(
                *(
                    over_heads(last_parts, group + half * (G // HALVES), spread[...])[7:8, :]
                    for half in range(HALVES)
                )
            )
            for at in here:
                lanes = slice(at * width, (at + 1) * width)
                states[local * len(here) + at, N:height, :] = pieces[:, lanes]


def within_kernel(first_group, x_in, b_in, c_in, step, decay, skip, out, running_all, steps_all):
    scores = dot(c_in[...], b_in[...], 1, 1)
    causal = lower_ones(scores.shape[0])
    @pl.when(pl.program_id(0) == 0)
    def _():
        running_all[...] = dot(decay[...], causal.astype(BF16), 0, 1)
        steps_all[...] = step[...].astype(F32).T

    group = first_group + pl.program_id(0)
    running = group_columns(running_sum(decay[...]), group)
    heads = pl.ds(pl.multiple_of(group * GROUP_HEADS, GROUP_HEADS), GROUP_HEADS)
    running_t = running_all[heads, :]
    steps = steps_all[heads, :]
    scores = jnp.where(causal, scores, 0.0)
    for pair in range(GROUP_HEADS // 2):
        parts = []
        x_pair = x_in[:, pair * 2 * P_SIZE : (pair + 1) * 2 * P_SIZE]
        for h in (2 * pair, 2 * pair + 1):
            gap = jnp.where(causal, running[:, h : h + 1] - running_t[h : h + 1, :], -jnp.inf)
            mix = (scores * jnp.exp(gap) * steps[h : h + 1, :]).astype(BF16)
            parts.append(dot(mix, x_pair[:, (h % 2) * P_SIZE : (h % 2 + 1) * P_SIZE], 1, 0))
        at = slice(pair * 2 * P_SIZE, (pair + 1) * 2 * P_SIZE)
        out[:, at] = jnp.concatenate(parts, axis=1) + skip[:, at] * x_pair.astype(F32)


def chunk_decays(decays, half):
    return jnp.sum(decays[:, 3 * half : 3 * half + 3, :].astype(F32), axis=1)


def section_total_kernel(half, states, decays, total):
    chunks = states.shape[0]
    sums = chunk_decays(decays, half)
    gains = jnp.exp(sums)
    for part in range(N // 32):
        at = slice(part * 32, (part + 1) * 32)
        carried = states[0, at, :].astype(F32)
        for chunk in range(1, chunks):
            carried = gains[chunk : chunk + 1, :] * carried + states[chunk, at, :].astype(F32)
        total[at, :] = carried.astype(BF16)
    total[N : N + 8, :] = decay_rows(jnp.sum(sums, axis=0, keepdims=True))


def entering_kernel(half, states, decays, totals, entering):
    chunks = states.shape[0]
    sections = totals.shape[0]
    here = lax.axis_index("sec")
    gains = jnp.exp(chunk_decays(decays, half))
    section_gains = jnp.exp(chunk_decays(totals[:, N : N + 8, :], 0))
    for part in range(N // 32):
        at = slice(part * 32, (part + 1) * 32)
        carried = jnp.zeros((32, states.shape[2]), F32)
        for section in range(sections - 1):
            after = section_gains[section : section + 1, :] * carried
            after = after + totals[section, at, :].astype(F32)
            carried = jnp.where(section < here, after, carried)
        for chunk in range(chunks):
            entering[chunk, at, :] = carried.astype(BF16)
            carried = gains[chunk : chunk + 1, :] * carried + states[chunk, at, :].astype(F32)


def outputs_kernel(first_group, within, c_in, decay, entering, *rest):
    out, spread = rest[-2:]
    groups = out.shape[1] // GROUP_WIDTH
    targets, _, width = entering.shape
    growth_parts = three_parts(jnp.exp(running_sum(decay[...])))

    @pl.when(pl.program_id(0) == 0)
    def _():
        spread[...] = spread_matrix()

    for local in range(groups):
        group = first_group + pl.program_id(0) * groups + local
        growth = over_heads(growth_parts, group, spread[...])
        query_c = c_in[:, local * N : (local + 1) * N]
        for at in range(targets // groups):
            lanes = slice(at * width, (at + 1) * width)
            wide = slice(local * GROUP_WIDTH + at * width, local * GROUP_WIDTH + (at + 1) * width)
            carried = dot(query_c, entering[local * (targets // groups) + at], 1, 0)
            out[:, wide] = (within[:, wide] + growth[:, lanes] * carried).astype(BF16)


def per_device(projected, conv_weight, conv_bias, step_size, log_decay, skip_gain):
    targets = lax.axis_size("cp")
    sections = lax.axis_size("sec")
    rows = projected.shape[0]
    width_all = projected.shape[1]
    devices = targets * sections
    groups = G // HALVES
    width_half = groups * GROUP_WIDTH
    width_here = width_half // targets
    group_targets = GROUP_WIDTH // width_here

    rim = lax.ppermute(
        projected[rows - (KERNEL - 1) :],
        ("sec", "cp"),
        [(source, source + 1) for source in range(devices - 1)],
    )
    bias = conv_bias.reshape(1, width_all)
    skip_wide = jnp.repeat(skip_gain, P_SIZE).reshape(1, WIDTH_X)
    params = pltpu.CompilerParams(vmem_limit_bytes=16 * 2**20)
    b_first = WIDTH_X // N
    c_first = b_first + G

    def columns_spec(height, width, first=0):
        return pl.BlockSpec((height, width), lambda g: (0, first + g))

    per_token = pl.BlockSpec((rows, HEAD_COUNT), lambda g: (0, 0))
    def conv_states(half):
        at_once = CONV_GROUPS
        first = half * groups // at_once
        wide = at_once * GROUP_WIDTH
        narrow = at_once * N
        state_rows = N if half else N + 8

        def three(height):
            return [
                columns_spec(height, wide, first),
                columns_spec(height, narrow, b_first // at_once + first),
                columns_spec(height, narrow, c_first // at_once + first),
            ]

        return pl.pallas_call(
            functools.partial(conv_states_kernel, half * groups),
            grid=(groups // at_once,),
            in_specs=three(rows) + three(KERNEL - 1) + three(KERNEL) + three(1) + [per_token] * 2,
            out_specs=[
                columns_spec(rows, wide),
                columns_spec(rows, narrow),
                columns_spec(rows, narrow),
                pl.BlockSpec(
                    (at_once * group_targets, state_rows, width_here), lambda g: (g, 0, 0)
                ),
            ],
            out_shape=[
                pltpu.HBM((rows, width_half), BF16),
                pltpu.HBM((rows, groups * N), BF16),
                pltpu.HBM((rows, groups * N), BF16),
                pltpu.HBM((targets, state_rows, width_here), BF16),
            ],
            scratch_shapes=[pltpu.VMEM((HEAD_COUNT, GROUP_WIDTH), BF16)],
            compiler_params=params,
            name="conv_states",
        )(
            projected, projected, projected, rim, rim, rim, conv_weight, conv_weight, conv_weight,
            bias, bias, bias, step_size, log_decay,
        )

    def within_chunk(half, values, keys_b, query_c):
        first = half * groups
        return pl.pallas_call(
            functools.partial(within_kernel, first),
            grid=(groups,),
            in_specs=[
                columns_spec(rows, GROUP_WIDTH),
                columns_spec(rows, N),
                columns_spec(rows, N),
                per_token,
                per_token,
                columns_spec(1, GROUP_WIDTH, first),
            ],
            out_specs=columns_spec(rows, GROUP_WIDTH),
            out_shape=pltpu.HBM((rows, width_half), F32),
            scratch_shapes=[pltpu.VMEM((HEAD_COUNT, rows), F32)] * 2,
            compiler_params=params,
            name="within",
        )(values, keys_b, query_c, step_size, log_decay, skip_wide)

    arrived_specs = [
        pl.BlockSpec((targets, N, width_here), lambda g: (0, 0, 0)),
        pl.BlockSpec((targets, 8, width_here), lambda g: (0, N // 8, 0)),
    ]
    total_spec = pl.BlockSpec((N + 8, width_here), lambda g: (0, 0))

    def section_total(half, states, first_states):
        return pl.pallas_call(
            functools.partial(section_total_kernel, half),
            grid=(1,),
            in_specs=arrived_specs,
            out_specs=total_spec,
            out_shape=jax.ShapeDtypeStruct((N + 8, width_here), BF16),
            compiler_params=params,
            name="section_total",
        )(states, first_states)

    def entering_states(half, states, first_states, totals):
        return pl.pallas_call(
            functools.partial(entering_kernel, half),
            grid=(1,),
            in_specs=arrived_specs
            + [pl.BlockSpec((sections, N + 8, width_here), lambda g: (0, 0, 0))],
            out_specs=pl.BlockSpec((targets, N, width_here), lambda g: (0, 0, 0)),
            out_shape=pltpu.HBM((targets, N, width_here), BF16),
            compiler_params=params,
            name="entering",
        )(states, first_states, totals)

    def outputs(half, within, query_c, entering, so_far):
        at_once = OUTPUT_GROUPS
        wide = at_once * GROUP_WIDTH
        carried = [] if so_far is None else [so_far]
        return pl.pallas_call(
            functools.partial(outputs_kernel, half * groups),
            grid=(groups // at_once,),
            in_specs=[
                columns_spec(rows, wide),
                columns_spec(rows, at_once * N),
                per_token,
                pl.BlockSpec((at_once * group_targets, N, width_here), lambda g: (g, 0, 0)),
            ]
            + [pl.BlockSpec(memory_space=pl.ANY)] * len(carried),
            out_specs=columns_spec(rows, wide, half * groups // at_once),
            out_shape=jax.ShapeDtypeStruct((rows, WIDTH_X), BF16),
            input_output_aliases={4: 0} if carried else {},
            scratch_shapes=[pltpu.VMEM((HEAD_COUNT, GROUP_WIDTH), BF16)],
            compiler_params=params,
            name="outputs",
        )(within, query_c, log_decay, entering, *carried)

    def exchanged(value):
        return lax.all_to_all(value, "cp", split_axis=0, concat_axis=0, tiled=True)

    def in_hbm(values):
        return [pltpu.with_memory_space_constraint(value, pltpu.HBM) for value in values]

    projected, conv_weight, bias, step_size, log_decay, skip_wide = in_hbm(
        (projected, conv_weight, bias, step_size, log_decay, skip_wide)
    )
    convs = [in_hbm(conv_states(half)) for half in range(HALVES)]
    states = [exchanged(conv[3]) for conv in convs]
    withins = [within_chunk(half, *convs[half][:3]) for half in range(HALVES)]
    arrived = []
    leaving = None
    for half in range(HALVES):
        state = states[half]
        if half:
            state, leaving = lax.optimization_barrier((state, leaving))
            arrived.append(exchanged(leaving))
        totals = lax.all_gather(section_total(half, state, states[0]), "sec")
        leaving = entering_states(half, state, states[0], totals)
    if arrived:
        arrived[-1], leaving = lax.optimization_barrier((arrived[-1], leaving))
    arrived.append(exchanged(leaving))
    result = None
    for half in range(HALVES):
        result = outputs(half, withins[half], convs[half][2], arrived[half], result)
    return result


def solution(mesh):
    in_specs = (
        P(("sec", "cp"), None),
        P(),
        P(),
        P(("sec", "cp"), None),
        P(("sec", "cp"), None),
        P(),
    )
    out_specs = P(("sec", "cp"), None)
    return jax.shard_map(
        per_device, mesh=mesh, in_specs=in_specs, out_specs=out_specs, check_vma=False
    )
```

```python
import functools

import jax
import jax.numpy as jnp
from jax import lax
from jax.experimental import pallas as pl
from jax.experimental.pallas import tpu as pltpu
from jax.sharding import PartitionSpec as P

HEAD_COUNT = 128
P_SIZE = 64
N = 128
G = 8
KERNEL = 4
GROUP_HEADS = HEAD_COUNT // G
GROUP_WIDTH = GROUP_HEADS * P_SIZE
WIDTH_X = HEAD_COUNT * P_SIZE
F32 = jnp.float32
BF16 = jnp.bfloat16
HALVES = 2
CONV_GROUPS = 4
OUTPUT_GROUPS = 4


def lower_ones(rows):
    down = lax.broadcasted_iota(jnp.int32, (rows, rows), 0)
    across = lax.broadcasted_iota(jnp.int32, (rows, rows), 1)
    return down >= across


def dot(a, b, a_dim, b_dim):
    return lax.dot_general(a, b, (((a_dim,), (b_dim,)), ((), ())), preferred_element_type=F32)


def running_sum(decay):
    return dot(lower_ones(decay.shape[0]).astype(BF16), decay, 1, 0)


def group_columns(columns, group):
    heads = columns.shape[1]
    return pltpu.roll(columns, lax.rem(heads - group * GROUP_HEADS, heads), 1)[:, :GROUP_HEADS]


def three_parts(value):
    high = value.astype(BF16).astype(F32)
    middle = (value - high).astype(BF16).astype(F32)
    return high, middle, value - high - middle


def spread_matrix():
    row = lax.broadcasted_iota(jnp.int32, (HEAD_COUNT, GROUP_WIDTH), 0)
    lane = lax.broadcasted_iota(jnp.int32, (HEAD_COUNT, GROUP_WIDTH), 1)
    head = lax.rem(row, GROUP_HEADS)
    return ((lane // P_SIZE == head) & (row < 3 * GROUP_HEADS)).astype(BF16)


def over_heads(parts, group, spread):
    rows = parts[0].shape[0]
    lane = lax.broadcasted_iota(jnp.int32, (rows, HEAD_COUNT), 1)
    picked = jnp.zeros((rows, HEAD_COUNT), F32)
    for place, part in enumerate(parts):
        by = lax.rem(HEAD_COUNT + (place - group) * GROUP_HEADS, HEAD_COUNT)
        moved = pltpu.roll(part, by, 1)
        inside = (lane >= place * GROUP_HEADS) & (lane < (place + 1) * GROUP_HEADS)
        picked = jnp.where(inside, moved, picked)
    return dot(picked.astype(BF16), spread, 1, 0)


def taps(extended, weights):
    before = pltpu.roll(extended, 1, 0)
    earlier = pltpu.roll(weights[1:2, :] * extended + weights[0:1, :] * before, 2, 0)
    return (weights[3:4, :] * extended + weights[2:3, :] * before + earlier)[8:, :]


def conv_silu(columns, rim, weights, biases):
    width = columns.shape[1]
    top = jnp.concatenate([jnp.zeros((8 - (KERNEL - 1), width), F32), rim.astype(F32)], axis=0)
    if columns.dtype == F32:
        added = taps(jnp.concatenate([top, jnp.zeros((8, width), F32)], axis=0), weights)
        summed = jnp.concatenate([columns[:8, :] + added, columns[8:, :]], axis=0)
    else:
        summed = biases + taps(jnp.concatenate([top, columns.astype(F32)], axis=0), weights)
    return (summed / (1.0 + jnp.exp(-summed))).astype(BF16)


def conv_sums_kernel(x_in, b_in, c_in, x_w, b_w, c_w, x_bias, b_bias, c_bias, x_out, b_out, c_out):
    for columns, weights, biases, out in (
        (x_in, x_w, x_bias, x_out),
        (b_in, b_w, b_bias, b_out),
        (c_in, c_w, c_bias, c_out),
    ):
        for first in range(0, out.shape[1], N):
            at = slice(first, first + N)
            top = jnp.zeros((8, N), F32)
            extended = jnp.concatenate([top, columns[:, at].astype(F32)], axis=0)
            out[:, at] = biases[:, at] + taps(extended, weights[:, at])


def decay_rows(*totals):
    row = lax.broadcasted_iota(jnp.int32, (8, totals[0].shape[1]), 0)
    value = jnp.zeros(row.shape, F32)
    for which, total in enumerate(totals):
        for place, part in enumerate(three_parts(total)):
            value = jnp.where(row == 3 * which + place, part, value)
    return value.astype(BF16)


def decay_of(rows):
    return jnp.sum(rows.astype(F32), axis=0, keepdims=True)


def conv_states_kernel(
    first_group, x_in, b_in, c_in, x_rim, b_rim, c_rim, x_w, b_w, c_w, x_bias, b_bias, c_bias, step, decay,
    x_out, b_out, c_out, states, spread,
):
    rows = x_in.shape[0]
    groups = x_in.shape[1] // GROUP_WIDTH
    targets, height, width = states.shape
    running_all = running_sum(decay[...])
    weight_parts = three_parts(
        jnp.exp(running_all[rows - 1 : rows, :] - running_all) * step[...].astype(F32)
    )
    last_parts = three_parts(running_all[rows - 8 : rows, :])

    @pl.when(pl.program_id(0) == 0)
    def _():
        spread[...] = spread_matrix()

    for local in range(groups):
        group = first_group + pl.program_id(0) * groups + local
        wide = slice(local * GROUP_WIDTH, (local + 1) * GROUP_WIDTH)
        narrow = slice(local * N, (local + 1) * N)
        values = conv_silu(x_in[:, wide], x_rim[:, wide], x_w[:, wide], x_bias[:, wide])
        keys_b = conv_silu(b_in[:, narrow], b_rim[:, narrow], b_w[:, narrow], b_bias[:, narrow])
        query_c = conv_silu(c_in[:, narrow], c_rim[:, narrow], c_w[:, narrow], c_bias[:, narrow])
        x_out[:, wide] = values
        b_out[:, narrow] = keys_b
        c_out[:, narrow] = query_c
        weighted = (values.astype(F32) * over_heads(weight_parts, group, spread[...])).astype(BF16)
        summed = dot(keys_b, weighted, 0, 0).astype(BF16)
        here = range(targets // groups)
        for at in here:
            lanes = slice(at * width, (at + 1) * width)
            states[local * len(here) + at, 0:N, :] = summed[:, lanes]
        if height > N:
            pieces = decay_rows(
                *(
                    over_heads(last_parts, group + half * (G // HALVES), spread[...])[7:8, :]
                    for half in range(HALVES)
                )
            )
            for at in here:
                lanes = slice(at * width, (at + 1) * width)
                states[local * len(here) + at, N:height, :] = pieces[:, lanes]


def within_kernel(first_group, x_in, b_in, c_in, step, decay, skip, out, running_all, steps_all):
    scores = dot(c_in[...], b_in[...], 1, 1)
    causal = lower_ones(scores.shape[0])
    @pl.when(pl.program_id(0) == 0)
    def _():
        running_all[...] = dot(decay[...], causal.astype(BF16), 0, 1)
        steps_all[...] = step[...].astype(F32).T

    group = first_group + pl.program_id(0)
    running = group_columns(running_sum(decay[...]), group)
    heads = pl.ds(pl.multiple_of(group * GROUP_HEADS, GROUP_HEADS), GROUP_HEADS)
    running_t = running_all[heads, :]
    steps = steps_all[heads, :]
    scores = jnp.where(causal, scores, 0.0)
    for pair in range(GROUP_HEADS // 2):
        parts = []
        x_pair = x_in[:, pair * 2 * P_SIZE : (pair + 1) * 2 * P_SIZE]
        for h in (2 * pair, 2 * pair + 1):
            gap = jnp.where(causal, running[:, h : h + 1] - running_t[h : h + 1, :], -jnp.inf)
            mix = (scores * jnp.exp(gap) * steps[h : h + 1, :]).astype(BF16)
            parts.append(dot(mix, x_pair[:, (h % 2) * P_SIZE : (h % 2 + 1) * P_SIZE], 1, 0))
        at = slice(pair * 2 * P_SIZE, (pair + 1) * 2 * P_SIZE)
        out[:, at] = jnp.concatenate(parts, axis=1) + skip[:, at] * x_pair.astype(F32)


def chunk_decays(decays, half):
    return jnp.sum(decays[:, 3 * half : 3 * half + 3, :].astype(F32), axis=1)


def section_total_kernel(half, states, decays, total):
    chunks = states.shape[0]
    sums = chunk_decays(decays, half)
    gains = jnp.exp(sums)
    for part in range(N // 32):
        at = slice(part * 32, (part + 1) * 32)
        carried = states[0, at, :].astype(F32)
        for chunk in range(1, chunks):
            carried = gains[chunk : chunk + 1, :] * carried + states[chunk, at, :].astype(F32)
        total[at, :] = carried.astype(BF16)
    total[N : N + 8, :] = decay_rows(jnp.sum(sums, axis=0, keepdims=True))


def entering_kernel(half, states, decays, totals, entering):
    chunks = states.shape[0]
    sections = totals.shape[0]
    here = lax.axis_index("sec")
    gains = jnp.exp(chunk_decays(decays, half))
    section_gains = jnp.exp(chunk_decays(totals[:, N : N + 8, :], 0))
    for part in range(N // 32):
        at = slice(part * 32, (part + 1) * 32)
        carried = jnp.zeros((32, states.shape[2]), F32)
        for section in range(sections - 1):
            after = section_gains[section : section + 1, :] * carried
            after = after + totals[section, at, :].astype(F32)
            carried = jnp.where(section < here, after, carried)
        for chunk in range(chunks):
            entering[chunk, at, :] = carried.astype(BF16)
            carried = gains[chunk : chunk + 1, :] * carried + states[chunk, at, :].astype(F32)


def outputs_kernel(first_group, within, c_in, decay, entering, *rest):
    out, spread = rest[-2:]
    groups = out.shape[1] // GROUP_WIDTH
    targets, _, width = entering.shape
    growth_parts = three_parts(jnp.exp(running_sum(decay[...])))

    @pl.when(pl.program_id(0) == 0)
    def _():
        spread[...] = spread_matrix()

    for local in range(groups):
        group = first_group + pl.program_id(0) * groups + local
        growth = over_heads(growth_parts, group, spread[...])
        query_c = c_in[:, local * N : (local + 1) * N]
        for at in range(targets // groups):
            lanes = slice(at * width, (at + 1) * width)
            wide = slice(local * GROUP_WIDTH + at * width, local * GROUP_WIDTH + (at + 1) * width)
            carried = dot(query_c, entering[local * (targets // groups) + at], 1, 0)
            out[:, wide] = (within[:, wide] + growth[:, lanes] * carried).astype(BF16)


def per_device(projected, conv_weight, conv_bias, step_size, log_decay, skip_gain):
    targets = lax.axis_size("cp")
    sections = lax.axis_size("sec")
    rows = projected.shape[0]
    width_all = projected.shape[1]
    devices = targets * sections
    groups = G // HALVES
    width_half = groups * GROUP_WIDTH
    width_here = width_half // targets
    group_targets = GROUP_WIDTH // width_here

    rim = lax.ppermute(
        projected[rows - (KERNEL - 1) :],
        ("sec", "cp"),
        [(source, source + 1) for source in range(devices - 1)],
    )
    bias = conv_bias.reshape(1, width_all)
    skip_wide = jnp.repeat(skip_gain, P_SIZE).reshape(1, WIDTH_X)
    params = pltpu.CompilerParams(vmem_limit_bytes=16 * 2**20)
    b_first = WIDTH_X // N
    c_first = b_first + G

    def columns_spec(height, width, first=0):
        return pl.BlockSpec((height, width), lambda g: (0, first + g))

    per_token = pl.BlockSpec((rows, HEAD_COUNT), lambda g: (0, 0))
    def conv_states(half):
        at_once = CONV_GROUPS
        first = half * groups // at_once
        wide = at_once * GROUP_WIDTH
        narrow = at_once * N
        state_rows = N if half else N + 8

        def three(height):
            return [
                columns_spec(height, wide, first),
                columns_spec(height, narrow, b_first // at_once + first),
                columns_spec(height, narrow, c_first // at_once + first),
            ]

        tokens, token_specs = [projected] * 3, three(rows)
        if not half:
            token_specs = [
                columns_spec(rows, wide), columns_spec(rows, narrow), columns_spec(rows, narrow)
            ]
            tokens = pl.pallas_call(
                conv_sums_kernel,
                grid=(groups // at_once,),
                in_specs=three(rows) + three(KERNEL) + three(1),
                out_specs=token_specs,
                out_shape=[
                    jax.ShapeDtypeStruct((rows, width_half), F32),
                    jax.ShapeDtypeStruct((rows, groups * N), F32),
                    jax.ShapeDtypeStruct((rows, groups * N), F32),
                ],
                compiler_params=params,
                name="conv_sums",
            )(*[projected] * 3, *[conv_weight] * 3, *[bias] * 3)
        return pl.pallas_call(
            functools.partial(conv_states_kernel, half * groups),
            grid=(groups // at_once,),
            in_specs=token_specs + three(KERNEL - 1) + three(KERNEL) + three(1) + [per_token] * 2,
            out_specs=[
                columns_spec(rows, wide),
                columns_spec(rows, narrow),
                columns_spec(rows, narrow),
                pl.BlockSpec(
                    (at_once * group_targets, state_rows, width_here), lambda g: (g, 0, 0)
                ),
            ],
            out_shape=[
                pltpu.HBM((rows, width_half), BF16),
                pltpu.HBM((rows, groups * N), BF16),
                pltpu.HBM((rows, groups * N), BF16),
                pltpu.HBM((targets, state_rows, width_here), BF16),
            ],
            scratch_shapes=[pltpu.VMEM((HEAD_COUNT, GROUP_WIDTH), BF16)],
            compiler_params=params,
            name="conv_states",
        )(
            *tokens, *[rim] * 3, *[conv_weight] * 3, *[bias] * 3, step_size, log_decay
        )

    def within_chunk(half, values, keys_b, query_c):
        first = half * groups
        return pl.pallas_call(
            functools.partial(within_kernel, first),
            grid=(groups,),
            in_specs=[
                columns_spec(rows, GROUP_WIDTH),
                columns_spec(rows, N),
                columns_spec(rows, N),
                per_token,
                per_token,
                columns_spec(1, GROUP_WIDTH, first),
            ],
            out_specs=columns_spec(rows, GROUP_WIDTH),
            out_shape=pltpu.HBM((rows, width_half), F32),
            scratch_shapes=[pltpu.VMEM((HEAD_COUNT, rows), F32)] * 2,
            compiler_params=params,
            name="within",
        )(values, keys_b, query_c, step_size, log_decay, skip_wide)

    arrived_specs = [
        pl.BlockSpec((targets, N, width_here), lambda g: (0, 0, 0)),
        pl.BlockSpec((targets, 8, width_here), lambda g: (0, N // 8, 0)),
    ]
    total_spec = pl.BlockSpec((N + 8, width_here), lambda g: (0, 0))

    def section_total(half, states, first_states):
        return pl.pallas_call(
            functools.partial(section_total_kernel, half),
            grid=(1,),
            in_specs=arrived_specs,
            out_specs=total_spec,
            out_shape=jax.ShapeDtypeStruct((N + 8, width_here), BF16),
            compiler_params=params,
            name="section_total",
        )(states, first_states)

    def entering_states(half, states, first_states, totals):
        return pl.pallas_call(
            functools.partial(entering_kernel, half),
            grid=(1,),
            in_specs=arrived_specs
            + [pl.BlockSpec((sections, N + 8, width_here), lambda g: (0, 0, 0))],
            out_specs=pl.BlockSpec((targets, N, width_here), lambda g: (0, 0, 0)),
            out_shape=pltpu.HBM((targets, N, width_here), BF16),
            compiler_params=params,
            name="entering",
        )(states, first_states, totals)

    def outputs(half, within, query_c, entering, so_far):
        at_once = OUTPUT_GROUPS
        wide = at_once * GROUP_WIDTH
        carried = [] if so_far is None else [so_far]
        return pl.pallas_call(
            functools.partial(outputs_kernel, half * groups),
            grid=(groups // at_once,),
            in_specs=[
                columns_spec(rows, wide),
                columns_spec(rows, at_once * N),
                per_token,
                pl.BlockSpec((at_once * group_targets, N, width_here), lambda g: (g, 0, 0)),
            ]
            + [pl.BlockSpec(memory_space=pl.ANY)] * len(carried),
            out_specs=columns_spec(rows, wide, half * groups // at_once),
            out_shape=jax.ShapeDtypeStruct((rows, WIDTH_X), BF16),
            input_output_aliases={4: 0} if carried else {},
            scratch_shapes=[pltpu.VMEM((HEAD_COUNT, GROUP_WIDTH), BF16)],
            compiler_params=params,
            name="outputs",
        )(within, query_c, log_decay, entering, *carried)

    def exchanged(value):
        return lax.all_to_all(value, "cp", split_axis=0, concat_axis=0, tiled=True)

    def in_hbm(values):
        return [pltpu.with_memory_space_constraint(value, pltpu.HBM) for value in values]

    projected, conv_weight, bias, step_size, log_decay, skip_wide = in_hbm(
        (projected, conv_weight, bias, step_size, log_decay, skip_wide)
    )
    convs = [in_hbm(conv_states(half)) for half in range(HALVES)]
    states = [exchanged(conv[3]) for conv in convs]
    withins = [within_chunk(half, *convs[half][:3]) for half in range(HALVES)]
    arrived = []
    leaving = None
    for half in range(HALVES):
        state = states[half]
        if half:
            state, leaving = lax.optimization_barrier((state, leaving))
            arrived.append(exchanged(leaving))
        totals = lax.all_gather(section_total(half, state, states[0]), "sec")
        leaving = entering_states(half, state, states[0], totals)
    if arrived:
        arrived[-1], leaving = lax.optimization_barrier((arrived[-1], leaving))
    arrived.append(exchanged(leaving))
    result = None
    for half in range(HALVES):
        result = outputs(half, withins[half], convs[half][2], arrived[half], result)
    return result


def solution(mesh):
    in_specs = (
        P(("sec", "cp"), None),
        P(),
        P(),
        P(("sec", "cp"), None),
        P(("sec", "cp"), None),
        P(),
    )
    out_specs = P(("sec", "cp"), None)
    return jax.shard_map(
        per_device, mesh=mesh, in_specs=in_specs, out_specs=out_specs, check_vma=False
    )
```

```python
import functools

import jax
import jax.numpy as jnp
from jax import lax
from jax.experimental import pallas as pl
from jax.experimental.pallas import tpu as pltpu
from jax.sharding import PartitionSpec as P

HEAD_COUNT = 128
P_SIZE = 64
N = 128
G = 8
KERNEL = 4
GROUP_HEADS = HEAD_COUNT // G
GROUP_WIDTH = GROUP_HEADS * P_SIZE
WIDTH_X = HEAD_COUNT * P_SIZE
F32 = jnp.float32
BF16 = jnp.bfloat16
HALVES = 2
CONV_GROUPS = 4
OUTPUT_GROUPS = 4


def lower_ones(rows):
    down = lax.broadcasted_iota(jnp.int32, (rows, rows), 0)
    across = lax.broadcasted_iota(jnp.int32, (rows, rows), 1)
    return down >= across


def dot(a, b, a_dim, b_dim):
    return lax.dot_general(a, b, (((a_dim,), (b_dim,)), ((), ())), preferred_element_type=F32)


def running_sum(decay):
    return dot(lower_ones(decay.shape[0]).astype(BF16), decay, 1, 0)


def group_columns(columns, group):
    heads = columns.shape[1]
    return pltpu.roll(columns, lax.rem(heads - group * GROUP_HEADS, heads), 1)[:, :GROUP_HEADS]


def three_parts(value):
    high = value.astype(BF16).astype(F32)
    middle = (value - high).astype(BF16).astype(F32)
    return high, middle, value - high - middle


def spread_matrix():
    row = lax.broadcasted_iota(jnp.int32, (HEAD_COUNT, GROUP_WIDTH), 0)
    lane = lax.broadcasted_iota(jnp.int32, (HEAD_COUNT, GROUP_WIDTH), 1)
    head = lax.rem(row, GROUP_HEADS)
    return ((lane // P_SIZE == head) & (row < 3 * GROUP_HEADS)).astype(BF16)


def over_heads(parts, group, spread):
    rows = parts[0].shape[0]
    lane = lax.broadcasted_iota(jnp.int32, (rows, HEAD_COUNT), 1)
    picked = jnp.zeros((rows, HEAD_COUNT), F32)
    for place, part in enumerate(parts):
        by = lax.rem(HEAD_COUNT + (place - group) * GROUP_HEADS, HEAD_COUNT)
        moved = pltpu.roll(part, by, 1)
        inside = (lane >= place * GROUP_HEADS) & (lane < (place + 1) * GROUP_HEADS)
        picked = jnp.where(inside, moved, picked)
    return dot(picked.astype(BF16), spread, 1, 0)


def taps(extended, weights):
    before = pltpu.roll(extended, 1, 0)
    earlier = pltpu.roll(weights[1:2, :] * extended + weights[0:1, :] * before, 2, 0)
    return (weights[3:4, :] * extended + weights[2:3, :] * before + earlier)[8:, :]


def conv_silu(columns, rim, weights, biases):
    width = columns.shape[1]
    top = jnp.concatenate([jnp.zeros((8 - (KERNEL - 1), width), F32), rim.astype(F32)], axis=0)
    if columns.dtype == F32:
        added = taps(jnp.concatenate([top, jnp.zeros((8, width), F32)], axis=0), weights)
        summed = jnp.concatenate([columns[:8, :] + added, columns[8:, :]], axis=0)
    else:
        summed = biases + taps(jnp.concatenate([top, columns.astype(F32)], axis=0), weights)
    return (summed / (1.0 + jnp.exp(-summed))).astype(BF16)


def conv_sums_kernel(x_in, b_in, c_in, x_w, b_w, c_w, x_bias, b_bias, c_bias, x_out, b_out, c_out):
    for columns, weights, biases, out in (
        (x_in, x_w, x_bias, x_out),
        (b_in, b_w, b_bias, b_out),
        (c_in, c_w, c_bias, c_out),
    ):
        for first in range(0, out.shape[1], N):
            at = slice(first, first + N)
            top = jnp.zeros((8, N), F32)
            extended = jnp.concatenate([top, columns[:, at].astype(F32)], axis=0)
            out[:, at] = biases[:, at] + taps(extended, weights[:, at])


def decay_rows(*totals):
    row = lax.broadcasted_iota(jnp.int32, (8, totals[0].shape[1]), 0)
    value = jnp.zeros(row.shape, F32)
    for which, total in enumerate(totals):
        for place, part in enumerate(three_parts(total)):
            value = jnp.where(row == 3 * which + place, part, value)
    return value.astype(BF16)


def decay_of(rows):
    return jnp.sum(rows.astype(F32), axis=0, keepdims=True)


def conv_states_kernel(
    first_group, x_in, b_in, c_in, x_rim, b_rim, c_rim, x_w, b_w, c_w, x_bias, b_bias, c_bias, step, decay,
    x_out, b_out, c_out, states, spread,
):
    rows = x_in.shape[0]
    groups = x_in.shape[1] // GROUP_WIDTH
    targets, height, width = states.shape
    running_all = running_sum(decay[...])
    weight_parts = three_parts(
        jnp.exp(running_all[rows - 1 : rows, :] - running_all) * step[...].astype(F32)
    )
    last_parts = three_parts(running_all[rows - 8 : rows, :])

    @pl.when(pl.program_id(0) == 0)
    def _():
        spread[...] = spread_matrix()

    for local in range(groups):
        group = first_group + pl.program_id(0) * groups + local
        wide = slice(local * GROUP_WIDTH, (local + 1) * GROUP_WIDTH)
        narrow = slice(local * N, (local + 1) * N)
        values = conv_silu(x_in[:, wide], x_rim[:, wide], x_w[:, wide], x_bias[:, wide])
        keys_b = conv_silu(b_in[:, narrow], b_rim[:, narrow], b_w[:, narrow], b_bias[:, narrow])
        query_c = conv_silu(c_in[:, narrow], c_rim[:, narrow], c_w[:, narrow], c_bias[:, narrow])
        if x_out is not None:
            x_out[:, wide] = values
            b_out[:, narrow] = keys_b
            c_out[:, narrow] = query_c
        weighted = (values.astype(F32) * over_heads(weight_parts, group, spread[...])).astype(BF16)
        summed = dot(keys_b, weighted, 0, 0).astype(BF16)
        here = range(targets // groups)
        for at in here:
            lanes = slice(at * width, (at + 1) * width)
            states[local * len(here) + at, 0:N, :] = summed[:, lanes]
        if height > N:
            pieces = decay_rows(
                *(
                    over_heads(last_parts, group + half * (G // HALVES), spread[...])[7:8, :]
                    for half in range(HALVES)
                )
            )
            for at in here:
                lanes = slice(at * width, (at + 1) * width)
                states[local * len(here) + at, N:height, :] = pieces[:, lanes]


def states_only_kernel(first_group, *refs):
    conv_states_kernel(first_group, *refs[:-2], None, None, None, *refs[-2:])


def conv_kernel(
    x_in, b_in, c_in, x_rim, b_rim, c_rim, x_w, b_w, c_w, x_bias, b_bias, c_bias, x_out, b_out, c_out
):
    for columns, rim, weights, biases, out in (
        (x_in, x_rim, x_w, x_bias, x_out),
        (b_in, b_rim, b_w, b_bias, b_out),
        (c_in, c_rim, c_w, c_bias, c_out),
    ):
        for first in range(0, out.shape[1], N):
            at = slice(first, first + N)
            out[:, at] = conv_silu(columns[:, at], rim[:, at], weights[:, at], biases[:, at])


def within_kernel(first_group, x_in, b_in, c_in, step, decay, skip, out, running_all, steps_all):
    scores = dot(c_in[...], b_in[...], 1, 1)
    causal = lower_ones(scores.shape[0])
    @pl.when(pl.program_id(0) == 0)
    def _():
        running_all[...] = dot(decay[...], causal.astype(BF16), 0, 1)
        steps_all[...] = step[...].astype(F32).T

    group = first_group + pl.program_id(0)
    running = group_columns(running_sum(decay[...]), group)
    heads = pl.ds(pl.multiple_of(group * GROUP_HEADS, GROUP_HEADS), GROUP_HEADS)
    running_t = running_all[heads, :]
    steps = steps_all[heads, :]
    scores = jnp.where(causal, scores, 0.0)
    for pair in range(GROUP_HEADS // 2):
        parts = []
        x_pair = x_in[:, pair * 2 * P_SIZE : (pair + 1) * 2 * P_SIZE]
        for h in (2 * pair, 2 * pair + 1):
            gap = jnp.where(causal, running[:, h : h + 1] - running_t[h : h + 1, :], -jnp.inf)
            mix = (scores * jnp.exp(gap) * steps[h : h + 1, :]).astype(BF16)
            parts.append(dot(mix, x_pair[:, (h % 2) * P_SIZE : (h % 2 + 1) * P_SIZE], 1, 0))
        at = slice(pair * 2 * P_SIZE, (pair + 1) * 2 * P_SIZE)
        out[:, at] = jnp.concatenate(parts, axis=1) + skip[:, at] * x_pair.astype(F32)


def chunk_decays(decays, half):
    return jnp.sum(decays[:, 3 * half : 3 * half + 3, :].astype(F32), axis=1)


def section_total_kernel(half, states, decays, total):
    chunks = states.shape[0]
    sums = chunk_decays(decays, half)
    gains = jnp.exp(sums)
    for part in range(N // 32):
        at = slice(part * 32, (part + 1) * 32)
        carried = states[0, at, :].astype(F32)
        for chunk in range(1, chunks):
            carried = gains[chunk : chunk + 1, :] * carried + states[chunk, at, :].astype(F32)
        total[at, :] = carried.astype(BF16)
    total[N : N + 8, :] = decay_rows(jnp.sum(sums, axis=0, keepdims=True))


def entering_kernel(half, states, decays, totals, entering):
    chunks = states.shape[0]
    sections = totals.shape[0]
    here = lax.axis_index("sec")
    gains = jnp.exp(chunk_decays(decays, half))
    section_gains = jnp.exp(chunk_decays(totals[:, N : N + 8, :], 0))
    for part in range(N // 32):
        at = slice(part * 32, (part + 1) * 32)
        carried = jnp.zeros((32, states.shape[2]), F32)
        for section in range(sections - 1):
            after = section_gains[section : section + 1, :] * carried
            after = after + totals[section, at, :].astype(F32)
            carried = jnp.where(section < here, after, carried)
        for chunk in range(chunks):
            entering[chunk, at, :] = carried.astype(BF16)
            carried = gains[chunk : chunk + 1, :] * carried + states[chunk, at, :].astype(F32)


def outputs_kernel(first_group, within, c_in, decay, entering, *rest):
    out, spread = rest[-2:]
    groups = out.shape[1] // GROUP_WIDTH
    targets, _, width = entering.shape
    growth_parts = three_parts(jnp.exp(running_sum(decay[...])))

    @pl.when(pl.program_id(0) == 0)
    def _():
        spread[...] = spread_matrix()

    for local in range(groups):
        group = first_group + pl.program_id(0) * groups + local
        growth = over_heads(growth_parts, group, spread[...])
        query_c = c_in[:, local * N : (local + 1) * N]
        for at in range(targets // groups):
            lanes = slice(at * width, (at + 1) * width)
            wide = slice(local * GROUP_WIDTH + at * width, local * GROUP_WIDTH + (at + 1) * width)
            carried = dot(query_c, entering[local * (targets // groups) + at], 1, 0)
            out[:, wide] = (within[:, wide] + growth[:, lanes] * carried).astype(BF16)


def per_device(projected, conv_weight, conv_bias, step_size, log_decay, skip_gain):
    targets = lax.axis_size("cp")
    sections = lax.axis_size("sec")
    rows = projected.shape[0]
    width_all = projected.shape[1]
    devices = targets * sections
    groups = G // HALVES
    width_half = groups * GROUP_WIDTH
    width_here = width_half // targets
    group_targets = GROUP_WIDTH // width_here

    rim = lax.ppermute(
        projected[rows - (KERNEL - 1) :],
        ("sec", "cp"),
        [(source, source + 1) for source in range(devices - 1)],
    )
    bias = conv_bias.reshape(1, width_all)
    skip_wide = jnp.repeat(skip_gain, P_SIZE).reshape(1, WIDTH_X)
    params = pltpu.CompilerParams(vmem_limit_bytes=16 * 2**20)
    b_first = WIDTH_X // N
    c_first = b_first + G

    def columns_spec(height, width, first=0):
        return pl.BlockSpec((height, width), lambda g: (0, first + g))

    per_token = pl.BlockSpec((rows, HEAD_COUNT), lambda g: (0, 0))
    def conv_states(half):
        at_once = CONV_GROUPS
        first = half * groups // at_once
        wide = at_once * GROUP_WIDTH
        narrow = at_once * N
        state_rows = N if half else N + 8

        def three(height):
            return [
                columns_spec(height, wide, first),
                columns_spec(height, narrow, b_first // at_once + first),
                columns_spec(height, narrow, c_first // at_once + first),
            ]

        tokens, token_specs = [projected] * 3, three(rows)
        if not half:
            token_specs = [
                columns_spec(rows, wide), columns_spec(rows, narrow), columns_spec(rows, narrow)
            ]
            tokens = pl.pallas_call(
                conv_sums_kernel,
                grid=(groups // at_once,),
                in_specs=three(rows) + three(KERNEL) + three(1),
                out_specs=token_specs,
                out_shape=[
                    jax.ShapeDtypeStruct((rows, width_half), F32),
                    jax.ShapeDtypeStruct((rows, groups * N), F32),
                    jax.ShapeDtypeStruct((rows, groups * N), F32),
                ],
                compiler_params=params,
                name="conv_sums",
            )(*[projected] * 3, *[conv_weight] * 3, *[bias] * 3)
        conv_specs = [
            columns_spec(rows, wide), columns_spec(rows, narrow), columns_spec(rows, narrow)
        ]
        conv_shapes = [
            pltpu.HBM((rows, width_half), BF16),
            pltpu.HBM((rows, groups * N), BF16),
            pltpu.HBM((rows, groups * N), BF16),
        ]
        around_specs = three(KERNEL - 1) + three(KERNEL) + three(1)
        around = [*[rim] * 3, *[conv_weight] * 3, *[bias] * 3]
        convolved = []
        if not half:
            convolved = pl.pallas_call(
                conv_kernel,
                grid=(groups // at_once,),
                in_specs=three(rows) + around_specs,
                out_specs=conv_specs,
                out_shape=conv_shapes,
                compiler_params=params,
                name="conv",
            )(*[projected] * 3, *around)
        kernel = conv_states_kernel if half else states_only_kernel
        results = pl.pallas_call(
            functools.partial(kernel, half * groups),
            grid=(groups // at_once,),
            in_specs=token_specs + around_specs + [per_token] * 2,
            out_specs=(conv_specs if half else [])
            + [
                pl.BlockSpec(
                    (at_once * group_targets, state_rows, width_here), lambda g: (g, 0, 0)
                ),
            ],
            out_shape=(conv_shapes if half else [])
            + [pltpu.HBM((targets, state_rows, width_here), BF16)],
            scratch_shapes=[pltpu.VMEM((HEAD_COUNT, GROUP_WIDTH), BF16)],
            compiler_params=params,
            name="conv_states",
        )(*tokens, *around, step_size, log_decay)
        return [*convolved, *results]

    def within_chunk(half, values, keys_b, query_c):
        first = half * groups
        return pl.pallas_call(
            functools.partial(within_kernel, first),
            grid=(groups,),
            in_specs=[
                columns_spec(rows, GROUP_WIDTH),
                columns_spec(rows, N),
                columns_spec(rows, N),
                per_token,
                per_token,
                columns_spec(1, GROUP_WIDTH, first),
            ],
            out_specs=columns_spec(rows, GROUP_WIDTH),
            out_shape=pltpu.HBM((rows, width_half), F32),
            scratch_shapes=[pltpu.VMEM((HEAD_COUNT, rows), F32)] * 2,
            compiler_params=params,
            name="within",
        )(values, keys_b, query_c, step_size, log_decay, skip_wide)

    arrived_specs = [
        pl.BlockSpec((targets, N, width_here), lambda g: (0, 0, 0)),
        pl.BlockSpec((targets, 8, width_here), lambda g: (0, N // 8, 0)),
    ]
    total_spec = pl.BlockSpec((N + 8, width_here), lambda g: (0, 0))

    def section_total(half, states, first_states):
        return pl.pallas_call(
            functools.partial(section_total_kernel, half),
            grid=(1,),
            in_specs=arrived_specs,
            out_specs=total_spec,
            out_shape=jax.ShapeDtypeStruct((N + 8, width_here), BF16),
            compiler_params=params,
            name="section_total",
        )(states, first_states)

    def entering_states(half, states, first_states, totals):
        return pl.pallas_call(
            functools.partial(entering_kernel, half),
            grid=(1,),
            in_specs=arrived_specs
            + [pl.BlockSpec((sections, N + 8, width_here), lambda g: (0, 0, 0))],
            out_specs=pl.BlockSpec((targets, N, width_here), lambda g: (0, 0, 0)),
            out_shape=pltpu.HBM((targets, N, width_here), BF16),
            compiler_params=params,
            name="entering",
        )(states, first_states, totals)

    def outputs(half, within, query_c, entering, so_far):
        at_once = OUTPUT_GROUPS
        wide = at_once * GROUP_WIDTH
        carried = [] if so_far is None else [so_far]
        return pl.pallas_call(
            functools.partial(outputs_kernel, half * groups),
            grid=(groups // at_once,),
            in_specs=[
                columns_spec(rows, wide),
                columns_spec(rows, at_once * N),
                per_token,
                pl.BlockSpec((at_once * group_targets, N, width_here), lambda g: (g, 0, 0)),
            ]
            + [pl.BlockSpec(memory_space=pl.ANY)] * len(carried),
            out_specs=columns_spec(rows, wide, half * groups // at_once),
            out_shape=jax.ShapeDtypeStruct((rows, WIDTH_X), BF16),
            input_output_aliases={4: 0} if carried else {},
            scratch_shapes=[pltpu.VMEM((HEAD_COUNT, GROUP_WIDTH), BF16)],
            compiler_params=params,
            name="outputs",
        )(within, query_c, log_decay, entering, *carried)

    def exchanged(value):
        return lax.all_to_all(value, "cp", split_axis=0, concat_axis=0, tiled=True)

    def in_hbm(values):
        return [pltpu.with_memory_space_constraint(value, pltpu.HBM) for value in values]

    projected, conv_weight, bias, step_size, log_decay, skip_wide = in_hbm(
        (projected, conv_weight, bias, step_size, log_decay, skip_wide)
    )
    convs = [in_hbm(conv_states(half)) for half in range(HALVES)]
    states = [exchanged(conv[3]) for conv in convs]
    withins = [within_chunk(half, *convs[half][:3]) for half in range(HALVES)]
    arrived = []
    leaving = None
    for half in range(HALVES):
        state = states[half]
        if half:
            state, leaving = lax.optimization_barrier((state, leaving))
            arrived.append(exchanged(leaving))
        totals = lax.all_gather(section_total(half, state, states[0]), "sec")
        leaving = entering_states(half, state, states[0], totals)
    if arrived:
        arrived[-1], leaving = lax.optimization_barrier((arrived[-1], leaving))
    arrived.append(exchanged(leaving))
    result = None
    for half in range(HALVES):
        result = outputs(half, withins[half], convs[half][2], arrived[half], result)
    return result


def solution(mesh):
    in_specs = (
        P(("sec", "cp"), None),
        P(),
        P(),
        P(("sec", "cp"), None),
        P(("sec", "cp"), None),
        P(),
    )
    out_specs = P(("sec", "cp"), None)
    return jax.shard_map(
        per_device, mesh=mesh, in_specs=in_specs, out_specs=out_specs, check_vma=False
    )
```

```python
import functools

import jax
import jax.numpy as jnp
from jax import lax
from jax.experimental import pallas as pl
from jax.experimental.pallas import tpu as pltpu
from jax.sharding import PartitionSpec as P

HEAD_COUNT = 128
P_SIZE = 64
N = 128
G = 8
KERNEL = 4
GROUP_HEADS = HEAD_COUNT // G
GROUP_WIDTH = GROUP_HEADS * P_SIZE
WIDTH_X = HEAD_COUNT * P_SIZE
F32 = jnp.float32
BF16 = jnp.bfloat16
HALVES = 2
CONV_GROUPS = 4
OUTPUT_GROUPS = 4


def lower_ones(rows):
    down = lax.broadcasted_iota(jnp.int32, (rows, rows), 0)
    across = lax.broadcasted_iota(jnp.int32, (rows, rows), 1)
    return down >= across


def dot(a, b, a_dim, b_dim):
    return lax.dot_general(a, b, (((a_dim,), (b_dim,)), ((), ())), preferred_element_type=F32)


def running_sum(decay):
    return dot(lower_ones(decay.shape[0]).astype(BF16), decay, 1, 0)


def group_columns(columns, group):
    heads = columns.shape[1]
    return pltpu.roll(columns, lax.rem(heads - group * GROUP_HEADS, heads), 1)[:, :GROUP_HEADS]


def three_parts(value):
    high = value.astype(BF16).astype(F32)
    middle = (value - high).astype(BF16).astype(F32)
    return high, middle, value - high - middle


def spread_matrix():
    row = lax.broadcasted_iota(jnp.int32, (HEAD_COUNT, GROUP_WIDTH), 0)
    lane = lax.broadcasted_iota(jnp.int32, (HEAD_COUNT, GROUP_WIDTH), 1)
    head = lax.rem(row, GROUP_HEADS)
    return ((lane // P_SIZE == head) & (row < 3 * GROUP_HEADS)).astype(BF16)


def over_heads(parts, group, spread):
    rows = parts[0].shape[0]
    lane = lax.broadcasted_iota(jnp.int32, (rows, HEAD_COUNT), 1)
    picked = jnp.zeros((rows, HEAD_COUNT), F32)
    for place, part in enumerate(parts):
        by = lax.rem(HEAD_COUNT + (place - group) * GROUP_HEADS, HEAD_COUNT)
        moved = pltpu.roll(part, by, 1)
        inside = (lane >= place * GROUP_HEADS) & (lane < (place + 1) * GROUP_HEADS)
        picked = jnp.where(inside, moved, picked)
    return dot(picked.astype(BF16), spread, 1, 0)


def taps(extended, weights):
    before = pltpu.roll(extended, 1, 0)
    earlier = pltpu.roll(weights[1:2, :] * extended + weights[0:1, :] * before, 2, 0)
    return (weights[3:4, :] * extended + weights[2:3, :] * before + earlier)[8:, :]


def conv_silu(columns, rim, weights, biases):
    width = columns.shape[1]
    top = jnp.concatenate([jnp.zeros((8 - (KERNEL - 1), width), F32), rim.astype(F32)], axis=0)
    if columns.dtype == F32:
        added = taps(jnp.concatenate([top, jnp.zeros((8, width), F32)], axis=0), weights)
        summed = jnp.concatenate([columns[:8, :] + added, columns[8:, :]], axis=0)
    else:
        summed = biases + taps(jnp.concatenate([top, columns.astype(F32)], axis=0), weights)
    half = 0.5 * summed
    return (half * jnp.tanh(half) + half).astype(BF16)


def conv_sums_kernel(x_in, b_in, c_in, x_w, b_w, c_w, x_bias, b_bias, c_bias, x_out, b_out, c_out):
    for columns, weights, biases, out in (
        (x_in, x_w, x_bias, x_out),
        (b_in, b_w, b_bias, b_out),
        (c_in, c_w, c_bias, c_out),
    ):
        for first in range(0, out.shape[1], N):
            at = slice(first, first + N)
            top = jnp.zeros((8, N), F32)
            extended = jnp.concatenate([top, columns[:, at].astype(F32)], axis=0)
            out[:, at] = biases[:, at] + taps(extended, weights[:, at])


def decay_rows(*totals):
    row = lax.broadcasted_iota(jnp.int32, (8, totals[0].shape[1]), 0)
    value = jnp.zeros(row.shape, F32)
    for which, total in enumerate(totals):
        for place, part in enumerate(three_parts(total)):
            value = jnp.where(row == 3 * which + place, part, value)
    return value.astype(BF16)


def decay_of(rows):
    return jnp.sum(rows.astype(F32), axis=0, keepdims=True)


def conv_states_kernel(
    first_group, x_in, b_in, c_in, x_rim, b_rim, c_rim, x_w, b_w, c_w, x_bias, b_bias, c_bias, step, decay,
    x_out, b_out, c_out, states, spread,
):
    rows = x_in.shape[0]
    groups = x_in.shape[1] // GROUP_WIDTH
    targets, height, width = states.shape
    running_all = running_sum(decay[...])
    weight_parts = three_parts(
        jnp.exp(running_all[rows - 1 : rows, :] - running_all) * step[...].astype(F32)
    )
    last_parts = three_parts(running_all[rows - 8 : rows, :])

    @pl.when(pl.program_id(0) == 0)
    def _():
        spread[...] = spread_matrix()

    for local in range(groups):
        group = first_group + pl.program_id(0) * groups + local
        wide = slice(local * GROUP_WIDTH, (local + 1) * GROUP_WIDTH)
        narrow = slice(local * N, (local + 1) * N)
        values = conv_silu(x_in[:, wide], x_rim[:, wide], x_w[:, wide], x_bias[:, wide])
        keys_b = conv_silu(b_in[:, narrow], b_rim[:, narrow], b_w[:, narrow], b_bias[:, narrow])
        query_c = conv_silu(c_in[:, narrow], c_rim[:, narrow], c_w[:, narrow], c_bias[:, narrow])
        if x_out is not None:
            x_out[:, wide] = values
            b_out[:, narrow] = keys_b
            c_out[:, narrow] = query_c
        weighted = (values.astype(F32) * over_heads(weight_parts, group, spread[...])).astype(BF16)
        summed = dot(keys_b, weighted, 0, 0).astype(BF16)
        here = range(targets // groups)
        for at in here:
            lanes = slice(at * width, (at + 1) * width)
            states[local * len(here) + at, 0:N, :] = summed[:, lanes]
        if height > N:
            pieces = decay_rows(
                *(
                    over_heads(last_parts, group + half * (G // HALVES), spread[...])[7:8, :]
                    for half in range(HALVES)
                )
            )
            for at in here:
                lanes = slice(at * width, (at + 1) * width)
                states[local * len(here) + at, N:height, :] = pieces[:, lanes]


def states_only_kernel(first_group, *refs):
    conv_states_kernel(first_group, *refs[:-2], None, None, None, *refs[-2:])


def conv_kernel(
    x_in, b_in, c_in, x_rim, b_rim, c_rim, x_w, b_w, c_w, x_bias, b_bias, c_bias, x_out, b_out, c_out
):
    for columns, rim, weights, biases, out in (
        (x_in, x_rim, x_w, x_bias, x_out),
        (b_in, b_rim, b_w, b_bias, b_out),
        (c_in, c_rim, c_w, c_bias, c_out),
    ):
        for first in range(0, out.shape[1], N):
            at = slice(first, first + N)
            out[:, at] = conv_silu(columns[:, at], rim[:, at], weights[:, at], biases[:, at])


def within_kernel(first_group, x_in, b_in, c_in, step, decay, skip, out, running_all, steps_all):
    scores = dot(c_in[...], b_in[...], 1, 1)
    causal = lower_ones(scores.shape[0])
    @pl.when(pl.program_id(0) == 0)
    def _():
        running_all[...] = dot(decay[...], causal.astype(BF16), 0, 1)
        steps_all[...] = step[...].astype(F32).T

    group = first_group + pl.program_id(0)
    running = group_columns(running_sum(decay[...]), group)
    heads = pl.ds(pl.multiple_of(group * GROUP_HEADS, GROUP_HEADS), GROUP_HEADS)
    running_t = running_all[heads, :]
    steps = steps_all[heads, :]
    scores = jnp.where(causal, scores, 0.0)
    for pair in range(GROUP_HEADS // 2):
        parts = []
        x_pair = x_in[:, pair * 2 * P_SIZE : (pair + 1) * 2 * P_SIZE]
        for h in (2 * pair, 2 * pair + 1):
            gap = jnp.where(causal, running[:, h : h + 1] - running_t[h : h + 1, :], -jnp.inf)
            mix = (scores * jnp.exp(gap) * steps[h : h + 1, :]).astype(BF16)
            parts.append(dot(mix, x_pair[:, (h % 2) * P_SIZE : (h % 2 + 1) * P_SIZE], 1, 0))
        at = slice(pair * 2 * P_SIZE, (pair + 1) * 2 * P_SIZE)
        out[:, at] = jnp.concatenate(parts, axis=1) + skip[:, at] * x_pair.astype(F32)


def chunk_decays(decays, half):
    return jnp.sum(decays[:, 3 * half : 3 * half + 3, :].astype(F32), axis=1)


def section_total_kernel(half, states, decays, total):
    chunks = states.shape[0]
    sums = chunk_decays(decays, half)
    gains = jnp.exp(sums)
    for part in range(N // 32):
        at = slice(part * 32, (part + 1) * 32)
        carried = states[0, at, :].astype(F32)
        for chunk in range(1, chunks):
            carried = gains[chunk : chunk + 1, :] * carried + states[chunk, at, :].astype(F32)
        total[at, :] = carried.astype(BF16)
    total[N : N + 8, :] = decay_rows(jnp.sum(sums, axis=0, keepdims=True))


def entering_kernel(half, states, decays, totals, entering):
    chunks = states.shape[0]
    sections = totals.shape[0]
    here = lax.axis_index("sec")
    gains = jnp.exp(chunk_decays(decays, half))
    section_gains = jnp.exp(chunk_decays(totals[:, N : N + 8, :], 0))
    for part in range(N // 32):
        at = slice(part * 32, (part + 1) * 32)
        carried = jnp.zeros((32, states.shape[2]), F32)
        for section in range(sections - 1):
            after = section_gains[section : section + 1, :] * carried
            after = after + totals[section, at, :].astype(F32)
            carried = jnp.where(section < here, after, carried)
        for chunk in range(chunks):
            entering[chunk, at, :] = carried.astype(BF16)
            carried = gains[chunk : chunk + 1, :] * carried + states[chunk, at, :].astype(F32)


def outputs_kernel(first_group, within, c_in, decay, entering, *rest):
    out, spread = rest[-2:]
    groups = out.shape[1] // GROUP_WIDTH
    targets, _, width = entering.shape
    growth_parts = three_parts(jnp.exp(running_sum(decay[...])))

    @pl.when(pl.program_id(0) == 0)
    def _():
        spread[...] = spread_matrix()

    for local in range(groups):
        group = first_group + pl.program_id(0) * groups + local
        growth = over_heads(growth_parts, group, spread[...])
        query_c = c_in[:, local * N : (local + 1) * N]
        for at in range(targets // groups):
            lanes = slice(at * width, (at + 1) * width)
            wide = slice(local * GROUP_WIDTH + at * width, local * GROUP_WIDTH + (at + 1) * width)
            carried = dot(query_c, entering[local * (targets // groups) + at], 1, 0)
            out[:, wide] = (within[:, wide] + growth[:, lanes] * carried).astype(BF16)


def per_device(projected, conv_weight, conv_bias, step_size, log_decay, skip_gain):
    targets = lax.axis_size("cp")
    sections = lax.axis_size("sec")
    rows = projected.shape[0]
    width_all = projected.shape[1]
    devices = targets * sections
    groups = G // HALVES
    width_half = groups * GROUP_WIDTH
    width_here = width_half // targets
    group_targets = GROUP_WIDTH // width_here

    rim = lax.ppermute(
        projected[rows - (KERNEL - 1) :],
        ("sec", "cp"),
        [(source, source + 1) for source in range(devices - 1)],
    )
    bias = conv_bias.reshape(1, width_all)
    skip_wide = jnp.repeat(skip_gain, P_SIZE).reshape(1, WIDTH_X)
    params = pltpu.CompilerParams(vmem_limit_bytes=16 * 2**20)
    b_first = WIDTH_X // N
    c_first = b_first + G

    def columns_spec(height, width, first=0):
        return pl.BlockSpec((height, width), lambda g: (0, first + g))

    per_token = pl.BlockSpec((rows, HEAD_COUNT), lambda g: (0, 0))
    def conv_states(half):
        at_once = CONV_GROUPS
        first = half * groups // at_once
        wide = at_once * GROUP_WIDTH
        narrow = at_once * N
        state_rows = N if half else N + 8

        def three(height):
            return [
                columns_spec(height, wide, first),
                columns_spec(height, narrow, b_first // at_once + first),
                columns_spec(height, narrow, c_first // at_once + first),
            ]

        tokens, token_specs = [projected] * 3, three(rows)
        if not half:
            token_specs = [
                columns_spec(rows, wide), columns_spec(rows, narrow), columns_spec(rows, narrow)
            ]
            tokens = pl.pallas_call(
                conv_sums_kernel,
                grid=(groups // at_once,),
                in_specs=three(rows) + three(KERNEL) + three(1),
                out_specs=token_specs,
                out_shape=[
                    jax.ShapeDtypeStruct((rows, width_half), F32),
                    jax.ShapeDtypeStruct((rows, groups * N), F32),
                    jax.ShapeDtypeStruct((rows, groups * N), F32),
                ],
                compiler_params=params,
                name="conv_sums",
            )(*[projected] * 3, *[conv_weight] * 3, *[bias] * 3)
        conv_specs = [
            columns_spec(rows, wide), columns_spec(rows, narrow), columns_spec(rows, narrow)
        ]
        conv_shapes = [
            pltpu.HBM((rows, width_half), BF16),
            pltpu.HBM((rows, groups * N), BF16),
            pltpu.HBM((rows, groups * N), BF16),
        ]
        around_specs = three(KERNEL - 1) + three(KERNEL) + three(1)
        around = [*[rim] * 3, *[conv_weight] * 3, *[bias] * 3]
        convolved = []
        if not half:
            convolved = pl.pallas_call(
                conv_kernel,
                grid=(groups // at_once,),
                in_specs=three(rows) + around_specs,
                out_specs=conv_specs,
                out_shape=conv_shapes,
                compiler_params=params,
                name="conv",
            )(*[projected] * 3, *around)
        kernel = conv_states_kernel if half else states_only_kernel
        results = pl.pallas_call(
            functools.partial(kernel, half * groups),
            grid=(groups // at_once,),
            in_specs=token_specs + around_specs + [per_token] * 2,
            out_specs=(conv_specs if half else [])
            + [
                pl.BlockSpec(
                    (at_once * group_targets, state_rows, width_here), lambda g: (g, 0, 0)
                ),
            ],
            out_shape=(conv_shapes if half else [])
            + [pltpu.HBM((targets, state_rows, width_here), BF16)],
            scratch_shapes=[pltpu.VMEM((HEAD_COUNT, GROUP_WIDTH), BF16)],
            compiler_params=params,
            name="conv_states",
        )(*tokens, *around, step_size, log_decay)
        return [*convolved, *results]

    def within_chunk(half, values, keys_b, query_c):
        first = half * groups
        return pl.pallas_call(
            functools.partial(within_kernel, first),
            grid=(groups,),
            in_specs=[
                columns_spec(rows, GROUP_WIDTH),
                columns_spec(rows, N),
                columns_spec(rows, N),
                per_token,
                per_token,
                columns_spec(1, GROUP_WIDTH, first),
            ],
            out_specs=columns_spec(rows, GROUP_WIDTH),
            out_shape=pltpu.HBM((rows, width_half), F32),
            scratch_shapes=[pltpu.VMEM((HEAD_COUNT, rows), F32)] * 2,
            compiler_params=params,
            name="within",
        )(values, keys_b, query_c, step_size, log_decay, skip_wide)

    arrived_specs = [
        pl.BlockSpec((targets, N, width_here), lambda g: (0, 0, 0)),
        pl.BlockSpec((targets, 8, width_here), lambda g: (0, N // 8, 0)),
    ]
    total_spec = pl.BlockSpec((N + 8, width_here), lambda g: (0, 0))

    def section_total(half, states, first_states):
        return pl.pallas_call(
            functools.partial(section_total_kernel, half),
            grid=(1,),
            in_specs=arrived_specs,
            out_specs=total_spec,
            out_shape=jax.ShapeDtypeStruct((N + 8, width_here), BF16),
            compiler_params=params,
            name="section_total",
        )(states, first_states)

    def entering_states(half, states, first_states, totals):
        return pl.pallas_call(
            functools.partial(entering_kernel, half),
            grid=(1,),
            in_specs=arrived_specs
            + [pl.BlockSpec((sections, N + 8, width_here), lambda g: (0, 0, 0))],
            out_specs=pl.BlockSpec((targets, N, width_here), lambda g: (0, 0, 0)),
            out_shape=pltpu.HBM((targets, N, width_here), BF16),
            compiler_params=params,
            name="entering",
        )(states, first_states, totals)

    def outputs(half, within, query_c, entering, so_far):
        at_once = OUTPUT_GROUPS
        wide = at_once * GROUP_WIDTH
        carried = [] if so_far is None else [so_far]
        return pl.pallas_call(
            functools.partial(outputs_kernel, half * groups),
            grid=(groups // at_once,),
            in_specs=[
                columns_spec(rows, wide),
                columns_spec(rows, at_once * N),
                per_token,
                pl.BlockSpec((at_once * group_targets, N, width_here), lambda g: (g, 0, 0)),
            ]
            + [pl.BlockSpec(memory_space=pl.ANY)] * len(carried),
            out_specs=columns_spec(rows, wide, half * groups // at_once),
            out_shape=jax.ShapeDtypeStruct((rows, WIDTH_X), BF16),
            input_output_aliases={4: 0} if carried else {},
            scratch_shapes=[pltpu.VMEM((HEAD_COUNT, GROUP_WIDTH), BF16)],
            compiler_params=params,
            name="outputs",
        )(within, query_c, log_decay, entering, *carried)

    def exchanged(value):
        return lax.all_to_all(value, "cp", split_axis=0, concat_axis=0, tiled=True)

    def in_hbm(values):
        return [pltpu.with_memory_space_constraint(value, pltpu.HBM) for value in values]

    projected, conv_weight, bias, step_size, log_decay, skip_wide = in_hbm(
        (projected, conv_weight, bias, step_size, log_decay, skip_wide)
    )
    convs = [in_hbm(conv_states(half)) for half in range(HALVES)]
    states = [exchanged(conv[3]) for conv in convs]
    withins = [within_chunk(half, *convs[half][:3]) for half in range(HALVES)]
    arrived = []
    leaving = None
    for half in range(HALVES):
        state = states[half]
        if half:
            state, leaving = lax.optimization_barrier((state, leaving))
            arrived.append(exchanged(leaving))
        totals = lax.all_gather(section_total(half, state, states[0]), "sec")
        leaving = entering_states(half, state, states[0], totals)
    if arrived:
        arrived[-1], leaving = lax.optimization_barrier((arrived[-1], leaving))
    arrived.append(exchanged(leaving))
    result = None
    for half in range(HALVES):
        result = outputs(half, withins[half], convs[half][2], arrived[half], result)
    return result


def solution(mesh):
    in_specs = (
        P(("sec", "cp"), None),
        P(),
        P(),
        P(("sec", "cp"), None),
        P(("sec", "cp"), None),
        P(),
    )
    out_specs = P(("sec", "cp"), None)
    return jax.shard_map(
        per_device, mesh=mesh, in_specs=in_specs, out_specs=out_specs, check_vma=False
    )
```
